256 devices in a mesh: circ: 64 (over z, y, core), ax: 4 (over x).
Axes of the slice: x: 4, y: 4, z: 8, core: 2. Of those that a mesh axis runs over, the one named last changes fastest.
Arguments:
- adjoint: float32 [5, 2048, 16, 512], P(None, 'circ', 'ax'), may hold values from -6 to 6
- source: float32 [5, 2048, 16, 512], P(None, 'circ', 'ax'), may hold values from -6 to 6
- step_size: float32 [2048, 16, 512], P('circ', 'ax'), may hold values from 0.3 to 3
- lengths: int32 [2048, 16], P('circ', 'ax'), may hold values from 128 to 512, as said below
- line_owner: int32 [4, 2048, 4, 1], P('ax', 'circ'), may hold values from 0 to 63; in each aligned block of 128 rows (0 to 127, 128 to 255, ..., all dimensions but the last counted through in order) at most 4 rows name the same one
- coupling: float32 [4, 5, 5], replicated, may hold values from -1.25 to 1.25
- lower_coef: bfloat16 [4, 16384, 5, 512], P('ax', 'circ'), may hold values from 0.5 to 0.99609375
- upper_coef: bfloat16 [4, 16384, 5, 512], P('ax', 'circ'), may hold values from 0.5 to 0.99609375
- pivot_inverse: bfloat16 [4, 16384, 25, 512], P('ax', 'circ'), may hold values from -0.1796875 to 0.1796875
Outputs:
- updated: float32 [5, 2048, 16, 512], P(None, 'circ', 'ax')
The draws below stay inside these ranges and needn't reach their ends.
Inputs may be any that keep to these rules, and one draw needn't show every extreme that they name: `lengths`: on every device some column has the full 512 points. `line_owner`: among the lines of one device at most 4 name the same owner, and this bound is reached.
All inputs are finite; a program needn't handle non-finite values.
Results may differ from the reference program's by a relative error of at most 0.0003.
Values may be sent and summed in bfloat16 or wider, within the bound.
A program may use at most 128 MiB of HBM per device.

```python
import math
import jax
import jax.numpy as jnp
import numpy as np
from jax import lax

FIELDS = 5
CC = 32
CA = 4
L = 512
NL = 128
CAP = 4
RECV = 256
NC = 2048
NA = 16
AXG = 4
SLOTS = 16384
N_CIRC = 64


def draw_lengths(key, part):
    split_keys = jax.random.split(key, 3)
    drawn_lengths = jax.random.randint(split_keys[0], (NC, NA), L // 4, L + 1)
    pick_circ = jax.random.randint(split_keys[1], (NC // CC, NA // CA), 0, CC)
    pick_axial = jax.random.randint(split_keys[2], (NC // CC, NA // CA), 0, CA)
    circ_index = jnp.arange(NC)[:, None]
    axial_index = jnp.arange(NA)[None, :]
    chosen_circ = pick_circ[circ_index // CC, axial_index // CA]
    chosen_axial = pick_axial[circ_index // CC, axial_index // CA]
    chosen = (circ_index % CC == chosen_circ) & (axial_index % CA == chosen_axial)
    return jnp.where(chosen, L, drawn_lengths).astype(jnp.int32)


def steps_of(rng, extent, cuts, low, top_value):
    level = 1.0
    for position, blocks in cuts:
        steps = jax.random.uniform(jax.random.fold_in(jax.random.fold_in(rng, 6), position), (blocks,), jnp.float32, low / len(cuts), top_value / len(cuts))
        level = level * jnp.repeat(jnp.exp(steps), extent[position] // blocks).reshape((-1,) + (1,) * (len(extent) - 1 - position))
    return level


def routed_block(rng, own, number, rows, number_of, top, limit, slope):
    ranking = jax.random.permutation(rng, number_of)
    crowded, usual = load_shares(number_of, rows * top, limit, slope, True), load_shares(number_of, rows * top, limit, slope, False)
    places = jnp.arange(number_of)

    def named(tallies, offset_by):
        used = int((tallies > 0).sum())
        fixed = max(1, used // 4)
        passed = fixed + (places - fixed + offset_by * (used - fixed)) % max(1, number_of - fixed)
        return jnp.zeros((number_of,), jnp.int32).at[ranking[jnp.where(places < fixed, places, passed)]].set(jnp.asarray(tallies, jnp.int32))

    tallies = jnp.where(number % 4 == 0, named(crowded, number // 4), named(usual, number - number // 4 - 1))
    mixed = jax.random.permutation(jax.random.fold_in(own, 3), number_of)
    source_of, sink = mixed[0:number_of // 2 * 2:2], mixed[1:number_of // 2 * 2:2]
    margin = jnp.minimum(tallies[source_of] - 1, limit - tallies[sink]) // 2
    margin = jnp.where((source_of == ranking[0]) | (sink == ranking[0]) | (tallies[sink] == 0), 0, jnp.maximum(margin, 0))
    passed = jax.random.randint(jax.random.fold_in(own, 4), (number_of // 2,), 0, 1 << 20) % (margin + 1)
    tallies = tallies.at[source_of].add(-passed).at[sink].add(passed)
    items = jnp.searchsorted(jnp.cumsum(tallies), jnp.arange(rows * top), side="right").astype(jnp.int32)
    table = items.reshape(top, rows).T
    table = table[jax.random.permutation(jax.random.fold_in(own, 1), rows)]
    offset_by = jax.random.randint(jax.random.fold_in(own, 2), (rows, 1), 0, top)
    return jnp.take_along_axis(table, (jnp.arange(top)[None, :] + offset_by) % top, axis=1)


def load_shares(count, total, bound, skew, full):
    loads = [(1 << 20) // math.isqrt(grade ** skew) + 1 for grade in range(1, count + 1)]
    largest = bound if full else min(bound, max(-(-total // count), total * loads[0] // sum(loads)))
    least = 1 if total - largest >= count - 1 else 0
    given, rest = [largest] + [least] * (count - 1), total - largest - least * (count - 1)
    while rest > 0:
        free = [i for i in range(1, count) if given[i] < largest] or [i for i in range(1, count) if given[i] < bound]
        pool, budget = sum([loads[i] for i in free]), rest
        for i in free:
            addition = min(bound - given[i], max(1, budget * loads[i] // pool), rest)
            given[i] = given[i] + addition
            rest = rest - addition
    return np.array(given)


def centred(own_key, shape, deviation, limit, pieces=(), kind=jnp.bfloat16):
    factor_of = steps_of(own_key, shape, pieces, -0.22, 0.18) if pieces else 1.0
    entries = jax.random.normal(own_key, shape, jnp.float32) * deviation * factor_of
    return jnp.minimum(jnp.maximum(entries, -limit), limit).astype(kind)


def setup_inputs(seed: int = 0) -> dict:
    seeds = jax.random.split(jax.random.key(seed), 10)
    adjoint = centred(seeds[0], (FIELDS, NC, NA, L), 1.0, 6.0, ((1, 64), (2, 4)), jnp.float32)
    source = centred(seeds[1], (FIELDS, NC, NA, L), 1.0, 6.0, ((1, 64), (2, 4)), jnp.float32)
    step_size = jnp.clip(jnp.exp(math.log(3.0) - 2.3025851 * jax.random.uniform(seeds[2], (NC, NA, L), jnp.float32) ** steps_of(seeds[2], (NC, NA, L), ((0, 64), (1, 4)), -0.2, 0.2)), 0.3, 3.0)
    lengths = draw_lengths(jax.random.fold_in(seeds[9], 71), 0)
    line_owner_keys = jax.random.split(jax.random.fold_in(seeds[4], 1), AXG * NC * CA // NL)
    line_owner_turns = jax.random.permutation(jax.random.fold_in(seeds[4], 3), AXG * NC * CA // NL)
    line_owner = jax.vmap(lambda own, number: routed_block(jax.random.fold_in(seeds[4], 2), own, number, NL, N_CIRC, 1, CAP, 1))(line_owner_keys, line_owner_turns).reshape((AXG, NC, CA, 1))
    coupling = centred(seeds[5], (4, FIELDS, FIELDS), 20 ** -0.5, 1.25, (), jnp.float32)
    lower_coef = jnp.clip(jnp.exp(math.log(0.99609375) - 0.6892333 * jax.random.uniform(seeds[6], (AXG, SLOTS, FIELDS, L), jnp.float32) ** steps_of(seeds[6], (AXG, SLOTS, FIELDS, L), ((0, 4), (1, 64)), -0.2, 0.2)), 0.5, 0.99609375).astype(jnp.bfloat16)
    upper_coef = jnp.clip(jnp.exp(math.log(0.99609375) - 0.6892333 * jax.random.uniform(seeds[7], (AXG, SLOTS, FIELDS, L), jnp.float32) ** steps_of(seeds[7], (AXG, SLOTS, FIELDS, L), ((0, 4), (1, 64)), -0.2, 0.2)), 0.5, 0.99609375).astype(jnp.bfloat16)
    pivot_inverse = centred(seeds[8], (AXG, SLOTS, FIELDS * FIELDS, L), 0.03, 0.1796875, ((0, 4), (1, 64)))
    return dict(adjoint=adjoint, source=source, step_size=step_size, lengths=lengths, line_owner=line_owner, coupling=coupling, lower_coef=lower_coef, upper_coef=upper_coef, pivot_inverse=pivot_inverse)


def linear_recurrence(coef, value):
    def combine(earlier, later):
        return (earlier[0] * later[0], later[0] * earlier[1] + later[1])
    return lax.associative_scan(combine, (coef, value), axis=2)[1]


def line_solve(right_side, line_lens, lower_rows, upper_rows, pivot_rows):
    batch_rows = right_side.shape[0]
    points = right_side.shape[2]
    positions = jnp.arange(points).astype(jnp.float32)
    active = (positions[None, :] < line_lens[:, None]).astype(jnp.float32)[:, None, :]
    forward_coef = -(lower_rows.astype(jnp.float32) * active)
    interim = linear_recurrence(forward_coef, right_side * active)
    blocks = pivot_rows.astype(jnp.float32).reshape(batch_rows, 5, 5, points)
    applied = jnp.sum(blocks * interim[:, None, :, :], axis=2)
    backward_coef = -(upper_rows.astype(jnp.float32) * active)
    solved = linear_recurrence(jnp.flip(backward_coef, 2), jnp.flip(applied * active, 2))
    return jnp.flip(solved, 2)


def explicit_residual(adjoint, source, step_size, coupling):
    eastern = jnp.roll(adjoint, -1, axis=1)
    western = jnp.roll(adjoint, 1, axis=1)
    padded = jnp.pad(adjoint, ((0, 0), (0, 0), (1, 1), (0, 0)))
    upward = padded[:, :, 2:]
    downward = padded[:, :, :-2]
    high = lax.Precision.HIGHEST
    coupled = jnp.einsum("fg,gcal->fcal", coupling[0], eastern, precision=high)
    coupled = coupled + jnp.einsum("fg,gcal->fcal", coupling[1], western, precision=high)
    coupled = coupled + jnp.einsum("fg,gcal->fcal", coupling[2], upward, precision=high)
    coupled = coupled + jnp.einsum("fg,gcal->fcal", coupling[3], downward, precision=high)
    return source - adjoint + step_size[None] * coupled


def reference(adjoint, source, step_size, lengths, line_owner, coupling, lower_coef, upper_coef, pivot_inverse):
    residual = explicit_residual(adjoint, source, step_size, coupling)
    right_lines = residual.reshape(FIELDS, NC, AXG, CA, L).transpose(2, 1, 3, 0, 4).reshape(AXG, NC * CA, FIELDS, L)
    group_lens = lengths.reshape(NC, AXG, CA).transpose(1, 0, 2).reshape(AXG, NC * CA).astype(jnp.float32)
    owners = line_owner[..., 0].reshape(AXG, N_CIRC, NL)
    matches = owners[..., :, None] == owners[..., None, :]
    before = jnp.arange(NL)[None, :] < jnp.arange(NL)[:, None]
    rank_in = jnp.sum(matches & before, axis=-1).astype(jnp.int32)
    senders = jnp.arange(N_CIRC).astype(jnp.int32)[None, :, None]
    slot_ids = (owners * RECV + senders * CAP + rank_in).reshape(AXG, NC * CA).astype(jnp.int32)

    def solve_group(packed):
        group_rhs, lens_here, lower_here, upper_here, pivot_here, slots_here = packed
        return line_solve(group_rhs, lens_here, jnp.take(lower_here, slots_here, axis=0),
                          jnp.take(upper_here, slots_here, axis=0), jnp.take(pivot_here, slots_here, axis=0))

    correction = lax.map(solve_group, (right_lines, group_lens, lower_coef, upper_coef, pivot_inverse, slot_ids))
    correction = correction.reshape(AXG, NC, CA, FIELDS, L).transpose(3, 1, 0, 2, 4).reshape(FIELDS, NC, NA, L)
    return adjoint + correction
```

```python
import functools

import jax
import jax.numpy as jnp
from jax import lax
from jax.experimental import pallas as pl
from jax.experimental.pallas import tpu as pltpu
from jax.sharding import PartitionSpec as P


def extended(block, sides, width, periodic):
    for axis, dim in sides:
        count = lax.axis_size(axis)
        forward = [(i, i + 1) for i in range(count - 1)]
        if periodic:
            forward.append((count - 1, 0))
        backward = [(target, source) for source, target in forward]
        low = lax.ppermute(
            lax.slice_in_dim(block, block.shape[dim] - width, None, axis=dim), axis, forward
        )
        high = lax.ppermute(lax.slice_in_dim(block, 0, width, axis=dim), axis, backward)
        block = jnp.concatenate([low, block, high], axis=dim)
    return block


def scan_forward(coef, value, pos):
    points = value.shape[-1]
    shift = 1
    while shift < points:
        keep = pos >= shift
        value = value + coef * jnp.where(keep, pltpu.roll(value, shift, 2), 0.0)
        coef = coef * pltpu.roll(coef, shift, 2)
        shift *= 2
    return value


def scan_backward(coef, value, pos):
    points = value.shape[-1]
    shift = 1
    while shift < points:
        keep = pos < points - shift
        value = value + coef * jnp.where(keep, pltpu.roll(value, points - shift, 2), 0.0)
        coef = coef * pltpu.roll(coef, points - shift, 2)
        shift *= 2
    return value


def solve_kernel(rhs_ref, lens_ref, lower_ref, upper_ref, pivot_ref, adj_ref, out_ref):
    fields, rows, points = rhs_ref.shape
    pos = lax.broadcasted_iota(jnp.int32, (fields, rows, points), 2)
    active = pos < lens_ref[...][None, :, :]
    forward_coef = jnp.where(active, -lower_ref[...].astype(jnp.float32), 0.0)
    interim = scan_forward(forward_coef, jnp.where(active, rhs_ref[...], 0.0), pos)
    applied = []
    for f in range(fields):
        total = pivot_ref[f * fields].astype(jnp.float32) * interim[0]
        for g in range(1, fields):
            total = total + pivot_ref[f * fields + g].astype(jnp.float32) * interim[g]
        applied.append(total)
    applied = jnp.stack(applied, axis=0)
    backward_coef = jnp.where(active, -upper_ref[...].astype(jnp.float32), 0.0)
    solved = scan_backward(backward_coef, jnp.where(active, applied, 0.0), pos)
    out_ref[...] = adj_ref[...] + solved


def line_solve(rhs, lens, lower, upper, pivot, adj, block_rows=16):
    fields, lines, points = rhs.shape
    blocks = pivot.shape[0]
    grid = (lines // block_rows,)
    field_spec = pl.BlockSpec((fields, block_rows, points), lambda i: (0, i, 0))
    return pl.pallas_call(
        solve_kernel,
        out_shape=jax.ShapeDtypeStruct(rhs.shape, jnp.float32),
        grid=grid,
        in_specs=[
            field_spec,
            pl.BlockSpec((block_rows, 1), lambda i: (i, 0)),
            field_spec,
            field_spec,
            pl.BlockSpec((blocks, block_rows, points), lambda i: (0, i, 0)),
            field_spec,
        ],
        out_specs=field_spec,
    )(rhs, lens, lower, upper, pivot, adj)


def per_device(
    adjoint, source, step_size, lengths, line_owner, coupling, lower_coef, upper_coef, pivot_inverse
):
    fields, circ_cells, axial_cells, points = adjoint.shape
    line_count = circ_cells * axial_cells
    circ_devices = lax.axis_size("circ")
    capacity = 2 * line_count // circ_devices
    circ_padded = extended(adjoint, (("circ", 1),), 1, True)
    axial_padded = extended(adjoint, (("ax", 2),), 1, False)
    neighbours = (
        circ_padded[:, 2:],
        circ_padded[:, :-2],
        axial_padded[:, :, 2:],
        axial_padded[:, :, :-2],
    )
    coupled = None
    for k, near in enumerate(neighbours):
        for g in range(fields):
            term = coupling[k, :, g][:, None, None, None] * near[g][None]
            coupled = term if coupled is None else coupled + term
    residual = source - adjoint + step_size[None] * coupled
    line_rhs = residual.reshape(fields, line_count, points)
    line_adj = adjoint.reshape(fields, line_count, points)
    line_lens = lengths.reshape(line_count, 1)
    targets = line_owner.reshape(line_count)
    ordinal = jnp.arange(line_count)
    earlier_same = (targets[:, None] == targets[None, :]) & (ordinal[None, :] < ordinal[:, None])
    slot_ids = targets * capacity + jnp.sum(earlier_same, axis=1)
    lower_here, upper_here, pivot_here = (
        lax.all_to_all(lower_coef[0], "circ", split_axis=0, concat_axis=0, tiled=True),
        lax.all_to_all(upper_coef[0], "circ", split_axis=0, concat_axis=0, tiled=True),
        lax.all_to_all(pivot_inverse[0], "circ", split_axis=0, concat_axis=0, tiled=True),
    )
    lower_rows = jnp.take(lower_here, slot_ids, axis=0).transpose(1, 0, 2)
    upper_rows = jnp.take(upper_here, slot_ids, axis=0).transpose(1, 0, 2)
    pivot_rows = jnp.take(pivot_here, slot_ids, axis=0).transpose(1, 0, 2)
    updated = line_solve(line_rhs, line_lens, lower_rows, upper_rows, pivot_rows, line_adj)
    return updated.reshape(fields, circ_cells, axial_cells, points)


def solution(mesh):
    placed = (
        P(None, "circ", "ax", None),
        P(None, "circ", "ax", None),
        P("circ", "ax", None),
        P("circ", "ax"),
        P("ax", "circ", None, None),
        P(),
        P("ax", "circ", None, None),
        P("ax", "circ", None, None),
        P("ax", "circ", None, None),
    )
    return jax.shard_map(
        per_device,
        mesh=mesh,
        in_specs=placed,
        out_specs=P(None, "circ", "ax", None),
        check_vma=False,
    )
```

```python
import functools

import jax
import jax.numpy as jnp
from jax import lax
from jax.experimental import pallas as pl
from jax.experimental.pallas import tpu as pltpu
from jax.sharding import PartitionSpec as P


def extended(block, sides, width, periodic):
    for axis, dim in sides:
        count = lax.axis_size(axis)
        forward = [(i, i + 1) for i in range(count - 1)]
        if periodic:
            forward.append((count - 1, 0))
        backward = [(target, source) for source, target in forward]
        low = lax.ppermute(
            lax.slice_in_dim(block, block.shape[dim] - width, None, axis=dim), axis, forward
        )
        high = lax.ppermute(lax.slice_in_dim(block, 0, width, axis=dim), axis, backward)
        block = jnp.concatenate([low, block, high], axis=dim)
    return block


def scan_forward(coef, value, pos):
    points = value.shape[-1]
    shift = 1
    while shift < points:
        keep = pos >= shift
        value = value + coef * jnp.where(keep, pltpu.roll(value, shift, 2), 0.0)
        coef = coef * pltpu.roll(coef, shift, 2)
        shift *= 2
    return value


def scan_backward(coef, value, pos):
    points = value.shape[-1]
    shift = 1
    while shift < points:
        keep = pos < points - shift
        value = value + coef * jnp.where(keep, pltpu.roll(value, points - shift, 2), 0.0)
        coef = coef * pltpu.roll(coef, points - shift, 2)
        shift *= 2
    return value


def solve_kernel(rhs_ref, lower_ref, upper_ref, pivot_ref, out_ref):
    fields, rows, points = rhs_ref.shape
    pos = lax.broadcasted_iota(jnp.int32, (fields, rows, points), 2)
    rhs = rhs_ref[...]
    active = rhs == rhs
    forward_coef = jnp.where(active, -lower_ref[...].astype(jnp.float32), 0.0)
    interim = scan_forward(forward_coef, jnp.where(active, rhs, 0.0), pos)
    applied = []
    for f in range(fields):
        total = pivot_ref[f * fields].astype(jnp.float32) * interim[0]
        for g in range(1, fields):
            total = total + pivot_ref[f * fields + g].astype(jnp.float32) * interim[g]
        applied.append(total)
    applied = jnp.stack(applied, axis=0)
    backward_coef = jnp.where(active, -upper_ref[...].astype(jnp.float32), 0.0)
    out_ref[...] = scan_backward(backward_coef, jnp.where(active, applied, 0.0), pos)


def line_solve(rhs, lower, upper, pivot, block_rows=16):
    fields, lines, points = rhs.shape
    blocks = pivot.shape[0]
    grid = (lines // block_rows,)
    field_spec = pl.BlockSpec((fields, block_rows, points), lambda i: (0, i, 0))
    return pl.pallas_call(
        solve_kernel,
        out_shape=jax.ShapeDtypeStruct(rhs.shape, jnp.float32),
        grid=grid,
        in_specs=[
            field_spec,
            field_spec,
            field_spec,
            pl.BlockSpec((blocks, block_rows, points), lambda i: (0, i, 0)),
        ],
        out_specs=field_spec,
    )(rhs, lower, upper, pivot)


def per_device(
    adjoint, source, step_size, lengths, line_owner, coupling, lower_coef, upper_coef, pivot_inverse
):
    fields, circ_cells, axial_cells, points = adjoint.shape
    line_count = circ_cells * axial_cells
    circ_devices = lax.axis_size("circ")
    capacity = 2 * line_count // circ_devices
    slot_count = lower_coef.shape[1]
    circ_padded = extended(adjoint, (("circ", 1),), 1, True)
    axial_padded = extended(adjoint, (("ax", 2),), 1, False)
    neighbours = (
        circ_padded[:, 2:],
        circ_padded[:, :-2],
        axial_padded[:, :, 2:],
        axial_padded[:, :, :-2],
    )
    coupled = None
    for k, near in enumerate(neighbours):
        for g in range(fields):
            term = coupling[k, :, g][:, None, None, None] * near[g][None]
            coupled = term if coupled is None else coupled + term
    residual = source - adjoint + step_size[None] * coupled
    active = jnp.arange(points)[None, None, None, :] < lengths[None, :, :, None]
    residual = jnp.where(active, residual, jnp.nan)
    line_rhs = residual.reshape(fields, line_count, points)
    targets = line_owner.reshape(line_count)
    ordinal = jnp.arange(line_count)
    earlier_same = (targets[:, None] == targets[None, :]) & (ordinal[None, :] < ordinal[:, None])
    slot_ids = targets * capacity + jnp.sum(earlier_same, axis=1)
    line_of_slot = jnp.full((slot_count,), line_count, jnp.int32).at[slot_ids].set(
        ordinal.astype(jnp.int32)
    )
    padded_rhs = jnp.concatenate(
        [line_rhs, jnp.full((fields, 1, points), jnp.nan, jnp.float32)], axis=1
    )
    outgoing = jnp.take(padded_rhs, line_of_slot, axis=1)
    owned_rhs = lax.all_to_all(outgoing, "circ", split_axis=1, concat_axis=1, tiled=True)
    owned_solution = line_solve(
        owned_rhs,
        lower_coef[0].transpose(1, 0, 2),
        upper_coef[0].transpose(1, 0, 2),
        pivot_inverse[0].transpose(1, 0, 2),
    )
    returned = lax.all_to_all(owned_solution, "circ", split_axis=1, concat_axis=1, tiled=True)
    correction = jnp.take(returned, slot_ids, axis=1)
    return adjoint + correction.reshape(fields, circ_cells, axial_cells, points)


def solution(mesh):
    placed = (
        P(None, "circ", "ax", None),
        P(None, "circ", "ax", None),
        P("circ", "ax", None),
        P("circ", "ax"),
        P("ax", "circ", None, None),
        P(),
        P("ax", "circ", None, None),
        P("ax", "circ", None, None),
        P("ax", "circ", None, None),
    )
    return jax.shard_map(
        per_device,
        mesh=mesh,
        in_specs=placed,
        out_specs=P(None, "circ", "ax", None),
        check_vma=False,
    )
```

```python
import functools

import jax
import jax.numpy as jnp
from jax import lax
from jax.experimental import pallas as pl
from jax.experimental.pallas import tpu as pltpu
from jax.sharding import PartitionSpec as P


def extended(block, sides, width, periodic):
    for axis, dim in sides:
        count = lax.axis_size(axis)
        forward = [(i, i + 1) for i in range(count - 1)]
        if periodic:
            forward.append((count - 1, 0))
        backward = [(target, source) for source, target in forward]
        low = lax.ppermute(
            lax.slice_in_dim(block, block.shape[dim] - width, None, axis=dim), axis, forward
        )
        high = lax.ppermute(lax.slice_in_dim(block, 0, width, axis=dim), axis, backward)
        block = jnp.concatenate([low, block, high], axis=dim)
    return block


def scan_forward(coef, value, pos):
    points = value.shape[-1]
    shift = 1
    while shift < points:
        keep = pos >= shift
        value = value + coef * jnp.where(keep, pltpu.roll(value, shift, 2), 0.0)
        coef = coef * pltpu.roll(coef, shift, 2)
        shift *= 2
    return value


def scan_backward(coef, value, pos):
    points = value.shape[-1]
    shift = 1
    while shift < points:
        keep = pos < points - shift
        value = value + coef * jnp.where(keep, pltpu.roll(value, points - shift, 2), 0.0)
        coef = coef * pltpu.roll(coef, points - shift, 2)
        shift *= 2
    return value


def solve_kernel(rhs_ref, lower_ref, upper_ref, pivot_ref, out_ref):
    fields, rows, points = rhs_ref.shape
    pos = lax.broadcasted_iota(jnp.int32, (fields, rows, points), 2)
    rhs = rhs_ref[...]
    active = rhs == rhs
    forward_coef = jnp.where(active, -lower_ref[...].astype(jnp.float32), 0.0)
    interim = scan_forward(forward_coef, jnp.where(active, rhs, 0.0), pos)
    applied = []
    for f in range(fields):
        total = pivot_ref[f * fields].astype(jnp.float32) * interim[0]
        for g in range(1, fields):
            total = total + pivot_ref[f * fields + g].astype(jnp.float32) * interim[g]
        applied.append(total)
    applied = jnp.stack(applied, axis=0)
    backward_coef = jnp.where(active, -upper_ref[...].astype(jnp.float32), 0.0)
    out_ref[...] = scan_backward(backward_coef, jnp.where(active, applied, 0.0), pos)


def line_solve(rhs, lower, upper, pivot, block_rows=16):
    fields, lines, points = rhs.shape
    blocks = pivot.shape[0]
    grid = (lines // block_rows,)
    field_spec = pl.BlockSpec((fields, block_rows, points), lambda i: (0, i, 0))
    return pl.pallas_call(
        solve_kernel,
        out_shape=jax.ShapeDtypeStruct(rhs.shape, jnp.float32),
        grid=grid,
        in_specs=[
            field_spec,
            field_spec,
            field_spec,
            pl.BlockSpec((blocks, block_rows, points), lambda i: (0, i, 0)),
        ],
        out_specs=field_spec,
    )(rhs, lower, upper, pivot)


MESH = pl.DeviceIdType.MESH


def exchange_kernel(x_ref, o_ref, send_sems, recv_sems, local_sem):
    peers = x_ref.shape[0]
    me = lax.axis_index("circ")
    plane = lax.axis_index("ax")
    barrier = pltpu.get_barrier_semaphore()

    def greet(i, carry):
        peer = lax.rem(me + i, peers)
        pl.semaphore_signal(barrier, inc=1, device_id=(peer, plane), device_id_type=MESH)
        return carry

    lax.fori_loop(1, peers, greet, 0)
    pl.semaphore_wait(barrier, peers - 1)
    local = pltpu.make_async_copy(x_ref.at[me], o_ref.at[me], local_sem)
    local.start()

    def outgoing(i):
        peer = lax.rem(me + i, peers)
        return pltpu.make_async_remote_copy(
            src_ref=x_ref.at[peer],
            dst_ref=o_ref.at[me],
            send_sem=send_sems.at[peer],
            recv_sem=recv_sems.at[me],
            device_id=(peer, plane),
            device_id_type=MESH,
        )

    def incoming(i):
        peer = lax.rem(me + peers - i, peers)
        return pltpu.make_async_remote_copy(
            src_ref=x_ref.at[me],
            dst_ref=o_ref.at[peer],
            send_sem=send_sems.at[me],
            recv_sem=recv_sems.at[peer],
            device_id=(peer, plane),
            device_id_type=MESH,
        )

    def start(i, carry):
        outgoing(i).start()
        return carry

    def finish(i, carry):
        outgoing(i).wait_send()
        incoming(i).wait_recv()
        return carry

    lax.fori_loop(1, peers, start, 0)
    local.wait()
    lax.fori_loop(1, peers, finish, 0)


def exchange(chunks, collective_id):
    peers = chunks.shape[0]
    return pl.pallas_call(
        exchange_kernel,
        out_shape=jax.ShapeDtypeStruct(chunks.shape, chunks.dtype),
        in_specs=[pl.BlockSpec(memory_space=pl.ANY)],
        out_specs=pl.BlockSpec(memory_space=pl.ANY),
        scratch_shapes=[
            pltpu.SemaphoreType.DMA((peers,)),
            pltpu.SemaphoreType.DMA((peers,)),
            pltpu.SemaphoreType.DMA(()),
        ],
        compiler_params=pltpu.CompilerParams(collective_id=collective_id, has_side_effects=True),
    )(chunks)


def to_chunks(rows, peers):
    fields, slots, points = rows.shape
    per_peer = slots // peers
    flat = rows.reshape(fields, peers, per_peer, points).transpose(1, 0, 2, 3)
    return flat.reshape(peers, fields * per_peer * points // 128, 128)


def from_chunks(chunks, fields, points):
    peers = chunks.shape[0]
    per_peer = chunks.shape[1] * 128 // (fields * points)
    rows = chunks.reshape(peers, fields, per_peer, points).transpose(1, 0, 2, 3)
    return rows.reshape(fields, peers * per_peer, points)


def per_device(
    adjoint, source, step_size, lengths, line_owner, coupling, lower_coef, upper_coef, pivot_inverse
):
    fields, circ_cells, axial_cells, points = adjoint.shape
    line_count = circ_cells * axial_cells
    circ_devices = lax.axis_size("circ")
    capacity = 2 * line_count // circ_devices
    slot_count = lower_coef.shape[1]
    circ_padded = extended(adjoint, (("circ", 1),), 1, True)
    axial_padded = extended(adjoint, (("ax", 2),), 1, False)
    neighbours = (
        circ_padded[:, 2:],
        circ_padded[:, :-2],
        axial_padded[:, :, 2:],
        axial_padded[:, :, :-2],
    )
    coupled = None
    for k, near in enumerate(neighbours):
        for g in range(fields):
            term = coupling[k, :, g][:, None, None, None] * near[g][None]
            coupled = term if coupled is None else coupled + term
    residual = source - adjoint + step_size[None] * coupled
    active = jnp.arange(points)[None, None, None, :] < lengths[None, :, :, None]
    residual = jnp.where(active, residual, jnp.nan)
    line_rhs = residual.reshape(fields, line_count, points)
    targets = line_owner.reshape(line_count)
    ordinal = jnp.arange(line_count)
    earlier_same = (targets[:, None] == targets[None, :]) & (ordinal[None, :] < ordinal[:, None])
    slot_ids = targets * capacity + jnp.sum(earlier_same, axis=1)
    line_of_slot = jnp.full((slot_count,), line_count, jnp.int32).at[slot_ids].set(
        ordinal.astype(jnp.int32)
    )
    padded_rhs = jnp.concatenate(
        [line_rhs, jnp.full((fields, 1, points), jnp.nan, jnp.float32)], axis=1
    )
    outgoing = jnp.take(padded_rhs, line_of_slot, axis=1)
    owned_rhs = from_chunks(exchange(to_chunks(outgoing, circ_devices), 0), fields, points)
    owned_solution = line_solve(
        owned_rhs,
        lower_coef[0].transpose(1, 0, 2),
        upper_coef[0].transpose(1, 0, 2),
        pivot_inverse[0].transpose(1, 0, 2),
    )
    returned = from_chunks(exchange(to_chunks(owned_solution, circ_devices), 1), fields, points)
    correction = jnp.take(returned, slot_ids, axis=1)
    return adjoint + correction.reshape(fields, circ_cells, axial_cells, points)


def solution(mesh):
    placed = (
        P(None, "circ", "ax", None),
        P(None, "circ", "ax", None),
        P("circ", "ax", None),
        P("circ", "ax"),
        P("ax", "circ", None, None),
        P(),
        P("ax", "circ", None, None),
        P("ax", "circ", None, None),
        P("ax", "circ", None, None),
    )
    return jax.shard_map(
        per_device,
        mesh=mesh,
        in_specs=placed,
        out_specs=P(None, "circ", "ax", None),
        check_vma=False,
    )
```

```python
import functools

import jax
import jax.numpy as jnp
from jax import lax
from jax.experimental import pallas as pl
from jax.experimental.pallas import tpu as pltpu
from jax.sharding import PartitionSpec as P


def extended(block, sides, width, periodic):
    for axis, dim in sides:
        count = lax.axis_size(axis)
        forward = [(i, i + 1) for i in range(count - 1)]
        if periodic:
            forward.append((count - 1, 0))
        backward = [(target, source) for source, target in forward]
        low = lax.ppermute(
            lax.slice_in_dim(block, block.shape[dim] - width, None, axis=dim), axis, forward
        )
        high = lax.ppermute(lax.slice_in_dim(block, 0, width, axis=dim), axis, backward)
        block = jnp.concatenate([low, block, high], axis=dim)
    return block


def scan_forward(coef, value, pos):
    points = value.shape[-1]
    shift = 1
    while shift < points:
        keep = pos >= shift
        value = value + coef * jnp.where(keep, pltpu.roll(value, shift, 2), 0.0)
        coef = coef * pltpu.roll(coef, shift, 2)
        shift *= 2
    return value


def scan_backward(coef, value, pos):
    points = value.shape[-1]
    shift = 1
    while shift < points:
        keep = pos < points - shift
        value = value + coef * jnp.where(keep, pltpu.roll(value, points - shift, 2), 0.0)
        coef = coef * pltpu.roll(coef, points - shift, 2)
        shift *= 2
    return value


def solve_kernel(rhs_ref, lower_ref, upper_ref, pivot_ref, out_ref):
    fields, rows, points = rhs_ref.shape
    pos = lax.broadcasted_iota(jnp.int32, (fields, rows, points), 2)
    rhs = rhs_ref[...]
    active = rhs == rhs
    forward_coef = jnp.where(active, -lower_ref[...].astype(jnp.float32), 0.0)
    interim = scan_forward(forward_coef, jnp.where(active, rhs, 0.0), pos)
    applied = []
    for f in range(fields):
        total = pivot_ref[f * fields].astype(jnp.float32) * interim[0]
        for g in range(1, fields):
            total = total + pivot_ref[f * fields + g].astype(jnp.float32) * interim[g]
        applied.append(total)
    applied = jnp.stack(applied, axis=0)
    backward_coef = jnp.where(active, -upper_ref[...].astype(jnp.float32), 0.0)
    out_ref[...] = scan_backward(backward_coef, jnp.where(active, applied, 0.0), pos)


def line_solve(rhs, lower, upper, pivot, block_rows=16):
    fields, lines, points = rhs.shape
    blocks = pivot.shape[0]
    grid = (lines // block_rows,)
    field_spec = pl.BlockSpec((fields, block_rows, points), lambda i: (0, i, 0))
    return pl.pallas_call(
        solve_kernel,
        out_shape=jax.ShapeDtypeStruct(rhs.shape, jnp.float32),
        grid=grid,
        in_specs=[
            field_spec,
            field_spec,
            field_spec,
            pl.BlockSpec((blocks, block_rows, points), lambda i: (0, i, 0)),
        ],
        out_specs=field_spec,
    )(rhs, lower, upper, pivot)


MESH = pl.DeviceIdType.MESH


def exchange_kernel(peers, x_ref, o_ref, send_sems, recv_sems, local_sem):
    width = x_ref.shape[1] // peers
    me = lax.axis_index("circ")
    plane = lax.axis_index("ax")
    barrier = pltpu.get_barrier_semaphore()

    def greet(i, carry):
        peer = lax.rem(me + i, peers)
        pl.semaphore_signal(barrier, inc=1, device_id=(peer, plane), device_id_type=MESH)
        return carry

    lax.fori_loop(1, peers, greet, 0)
    pl.semaphore_wait(barrier, peers - 1)
    own = pl.ds(me * width, width)
    local = pltpu.make_async_copy(x_ref.at[:, own], o_ref.at[:, own], local_sem)
    local.start()

    def outgoing(i):
        peer = lax.rem(me + i, peers)
        return pltpu.make_async_remote_copy(
            src_ref=x_ref.at[:, pl.ds(peer * width, width)],
            dst_ref=o_ref.at[:, pl.ds(me * width, width)],
            send_sem=send_sems.at[peer],
            recv_sem=recv_sems.at[me],
            device_id=(peer, plane),
            device_id_type=MESH,
        )

    def incoming(i):
        peer = lax.rem(me + peers - i, peers)
        return pltpu.make_async_remote_copy(
            src_ref=x_ref.at[:, pl.ds(me * width, width)],
            dst_ref=o_ref.at[:, pl.ds(peer * width, width)],
            send_sem=send_sems.at[me],
            recv_sem=recv_sems.at[peer],
            device_id=(peer, plane),
            device_id_type=MESH,
        )

    def start(i, carry):
        outgoing(i).start()
        return carry

    def finish(i, carry):
        outgoing(i).wait_send()
        incoming(i).wait_recv()
        return carry

    lax.fori_loop(1, peers, start, 0)
    local.wait()
    lax.fori_loop(1, peers, finish, 0)


def exchange(chunks, peers, collective_id):
    return pl.pallas_call(
        functools.partial(exchange_kernel, peers),
        out_shape=jax.ShapeDtypeStruct(chunks.shape, chunks.dtype),
        in_specs=[pl.BlockSpec(memory_space=pl.ANY)],
        out_specs=pl.BlockSpec(memory_space=pl.ANY),
        scratch_shapes=[
            pltpu.SemaphoreType.DMA((peers,)),
            pltpu.SemaphoreType.DMA((peers,)),
            pltpu.SemaphoreType.DMA(()),
        ],
        compiler_params=pltpu.CompilerParams(collective_id=collective_id, has_side_effects=True),
    )(chunks)


def per_device(
    adjoint, source, step_size, lengths, line_owner, coupling, lower_coef, upper_coef, pivot_inverse
):
    fields, circ_cells, axial_cells, points = adjoint.shape
    line_count = circ_cells * axial_cells
    circ_devices = lax.axis_size("circ")
    capacity = 2 * line_count // circ_devices
    slot_count = lower_coef.shape[1]
    circ_padded = extended(adjoint, (("circ", 1),), 1, True)
    axial_padded = extended(adjoint, (("ax", 2),), 1, False)
    neighbours = (
        circ_padded[:, 2:],
        circ_padded[:, :-2],
        axial_padded[:, :, 2:],
        axial_padded[:, :, :-2],
    )
    coupled = None
    for k, near in enumerate(neighbours):
        for g in range(fields):
            term = coupling[k, :, g][:, None, None, None] * near[g][None]
            coupled = term if coupled is None else coupled + term
    residual = source - adjoint + step_size[None] * coupled
    active = jnp.arange(points)[None, None, None, :] < lengths[None, :, :, None]
    residual = jnp.where(active, residual, jnp.nan)
    line_rhs = residual.reshape(fields, line_count, points)
    targets = line_owner.reshape(line_count)
    ordinal = jnp.arange(line_count)
    earlier_same = (targets[:, None] == targets[None, :]) & (ordinal[None, :] < ordinal[:, None])
    slot_ids = targets * capacity + jnp.sum(earlier_same, axis=1)
    line_of_slot = jnp.full((slot_count,), line_count, jnp.int32).at[slot_ids].set(
        ordinal.astype(jnp.int32)
    )
    padded_rhs = jnp.concatenate(
        [line_rhs, jnp.full((fields, 1, points), jnp.nan, jnp.float32)], axis=1
    )
    outgoing = jnp.take(padded_rhs, line_of_slot, axis=1)
    owned_rhs = exchange(outgoing, circ_devices, 0)
    owned_solution = line_solve(
        owned_rhs,
        lower_coef[0].transpose(1, 0, 2),
        upper_coef[0].transpose(1, 0, 2),
        pivot_inverse[0].transpose(1, 0, 2),
    )
    returned = exchange(owned_solution, circ_devices, 1)
    correction = jnp.take(returned, slot_ids, axis=1)
    return adjoint + correction.reshape(fields, circ_cells, axial_cells, points)


def solution(mesh):
    placed = (
        P(None, "circ", "ax", None),
        P(None, "circ", "ax", None),
        P("circ", "ax", None),
        P("circ", "ax"),
        P("ax", "circ", None, None),
        P(),
        P("ax", "circ", None, None),
        P("ax", "circ", None, None),
        P("ax", "circ", None, None),
    )
    return jax.shard_map(
        per_device,
        mesh=mesh,
        in_specs=placed,
        out_specs=P(None, "circ", "ax", None),
        check_vma=False,
    )
```

```python
import functools

import jax
import jax.numpy as jnp
from jax import lax
from jax.experimental import pallas as pl
from jax.experimental.pallas import tpu as pltpu
from jax.sharding import PartitionSpec as P


def extended(block, sides, width, periodic):
    for axis, dim in sides:
        count = lax.axis_size(axis)
        forward = [(i, i + 1) for i in range(count - 1)]
        if periodic:
            forward.append((count - 1, 0))
        backward = [(target, source) for source, target in forward]
        low = lax.ppermute(
            lax.slice_in_dim(block, block.shape[dim] - width, None, axis=dim), axis, forward
        )
        high = lax.ppermute(lax.slice_in_dim(block, 0, width, axis=dim), axis, backward)
        block = jnp.concatenate([low, block, high], axis=dim)
    return block


def scan_forward(coef, value, pos):
    points = value.shape[-1]
    shift = 1
    while shift < points:
        keep = pos >= shift
        value = value + coef * jnp.where(keep, pltpu.roll(value, shift, 2), 0.0)
        coef = coef * pltpu.roll(coef, shift, 2)
        shift *= 2
    return value


def scan_backward(coef, value, pos):
    points = value.shape[-1]
    shift = 1
    while shift < points:
        keep = pos < points - shift
        value = value + coef * jnp.where(keep, pltpu.roll(value, points - shift, 2), 0.0)
        coef = coef * pltpu.roll(coef, points - shift, 2)
        shift *= 2
    return value


MESH = pl.DeviceIdType.MESH


def exchange_kernel(peers, x_ref, o_ref, send_sems, recv_sems, local_sem):
    width = x_ref.shape[1] // peers
    me = lax.axis_index("circ")
    plane = lax.axis_index("ax")
    barrier = pltpu.get_barrier_semaphore()

    def greet(i, carry):
        peer = lax.rem(me + i, peers)
        pl.semaphore_signal(barrier, inc=1, device_id=(peer, plane), device_id_type=MESH)
        return carry

    lax.fori_loop(1, peers, greet, 0)
    pl.semaphore_wait(barrier, peers - 1)
    own = pl.ds(me * width, width)
    local = pltpu.make_async_copy(x_ref.at[:, own], o_ref.at[:, own], local_sem)
    local.start()

    def outgoing(i):
        peer = lax.rem(me + i, peers)
        return pltpu.make_async_remote_copy(
            src_ref=x_ref.at[:, pl.ds(peer * width, width)],
            dst_ref=o_ref.at[:, pl.ds(me * width, width)],
            send_sem=send_sems.at[peer],
            recv_sem=recv_sems.at[me],
            device_id=(peer, plane),
            device_id_type=MESH,
        )

    def incoming(i):
        peer = lax.rem(me + peers - i, peers)
        return pltpu.make_async_remote_copy(
            src_ref=x_ref.at[:, pl.ds(me * width, width)],
            dst_ref=o_ref.at[:, pl.ds(peer * width, width)],
            send_sem=send_sems.at[me],
            recv_sem=recv_sems.at[peer],
            device_id=(peer, plane),
            device_id_type=MESH,
        )

    def start(i, carry):
        outgoing(i).start()
        return carry

    def finish(i, carry):
        outgoing(i).wait_send()
        incoming(i).wait_recv()
        return carry

    lax.fori_loop(1, peers, start, 0)
    local.wait()
    lax.fori_loop(1, peers, finish, 0)


def exchange(chunks, peers, collective_id):
    return pl.pallas_call(
        functools.partial(exchange_kernel, peers),
        out_shape=jax.ShapeDtypeStruct(chunks.shape, chunks.dtype),
        in_specs=[pl.BlockSpec(memory_space=pl.ANY)],
        out_specs=pl.BlockSpec(memory_space=pl.ANY),
        scratch_shapes=[
            pltpu.SemaphoreType.DMA((peers,)),
            pltpu.SemaphoreType.DMA((peers,)),
            pltpu.SemaphoreType.DMA(()),
        ],
        compiler_params=pltpu.CompilerParams(collective_id=collective_id, has_side_effects=True),
    )(chunks)


def solve_rows(rhs, lower, upper, pivot):
    fields, rows, points = rhs.shape
    pos = lax.broadcasted_iota(jnp.int32, (fields, rows, points), 2)
    active = rhs == rhs
    forward_coef = jnp.where(active, -lower.astype(jnp.float32), 0.0)
    interim = scan_forward(forward_coef, jnp.where(active, rhs, 0.0), pos)
    applied = []
    for f in range(fields):
        total = pivot[f * fields].astype(jnp.float32) * interim[0]
        for g in range(1, fields):
            total = total + pivot[f * fields + g].astype(jnp.float32) * interim[g]
        applied.append(total)
    applied = jnp.stack(applied, axis=0)
    backward_coef = jnp.where(active, -upper.astype(jnp.float32), 0.0)
    return scan_backward(backward_coef, jnp.where(active, applied, 0.0), pos)


def owner_kernel(
    peers, group, rhs_ref, lower_ref, upper_ref, pivot_ref, out_ref,
    rhs_in, solved, lower_v, upper_v, pivot_v,
    send_rhs, recv_rhs, send_sol, recv_sol, local_sems,
):
    width = rhs_ref.shape[1] // peers
    groups = peers // group
    rows = group * width
    me = lax.axis_index("circ")
    plane = lax.axis_index("ax")
    mine = me // group
    factor_copies = [
        pltpu.make_async_copy(lower_ref, lower_v, local_sems.at[0]),
        pltpu.make_async_copy(upper_ref, upper_v, local_sems.at[1]),
        pltpu.make_async_copy(pivot_ref, pivot_v, local_sems.at[2]),
    ]
    for copy in factor_copies:
        copy.start()
    barrier = pltpu.get_barrier_semaphore()

    def greet(i, carry):
        peer = lax.rem(me + i, peers)
        pl.semaphore_signal(barrier, inc=1, device_id=(peer, plane), device_id_type=MESH)
        return carry

    lax.fori_loop(1, peers, greet, 0)
    pl.semaphore_wait(barrier, peers - 1)

    def window(index):
        return pl.ds(index * width, width)

    def rhs_copy(source, target):
        return pltpu.make_async_remote_copy(
            src_ref=rhs_ref.at[:, window(target)],
            dst_ref=rhs_in.at[:, window(source)],
            send_sem=send_rhs.at[target],
            recv_sem=recv_rhs.at[source],
            device_id=(lax.select(source == me, target, source), plane),
            device_id_type=MESH,
        )

    def sol_copy(source, target):
        return pltpu.make_async_remote_copy(
            src_ref=solved.at[:, window(target)],
            dst_ref=out_ref.at[:, window(source)],
            send_sem=send_sol.at[target],
            recv_sem=recv_sol.at[source],
            device_id=(lax.select(source == me, target, source), plane),
            device_id_type=MESH,
        )

    own_rhs = pltpu.make_async_copy(rhs_ref.at[:, window(me)], rhs_in.at[:, window(me)], local_sems.at[3])
    own_sol = pltpu.make_async_copy(solved.at[:, window(me)], out_ref.at[:, window(me)], local_sems.at[4])

    def send(i, carry):
        target = group * lax.rem(mine - i // group + groups, groups) + i % group

        @pl.when(target == me)
        def _():
            own_rhs.start()

        @pl.when(target != me)
        def _():
            rhs_copy(me, target).start()

        return carry

    lax.fori_loop(0, peers, send, 0)
    for copy in factor_copies:
        copy.wait()

    def solve(j, carry):
        g = lax.rem(mine + j, groups)
        for r in range(group):
            source = g * group + r

            @pl.when(source == me)
            def _():
                own_rhs.wait()

            @pl.when(source != me)
            def _():
                rhs_copy(source, me).wait_recv()

        block = pl.ds(pl.multiple_of(g * rows, rows), rows)
        solved[:, block, :] = solve_rows(
            rhs_in[:, block, :], lower_v[:, block, :], upper_v[:, block, :], pivot_v[:, block, :]
        )
        for r in range(group):
            target = g * group + r

            @pl.when(target == me)
            def _():
                own_sol.start()

            @pl.when(target != me)
            def _():
                sol_copy(me, target).start()

        return carry

    lax.fori_loop(0, groups, solve, 0)

    def finish(i, carry):
        peer = lax.rem(me + i, peers)
        rhs_copy(me, peer).wait_send()
        sol_copy(me, peer).wait_send()
        sol_copy(peer, me).wait_recv()
        return carry

    lax.fori_loop(1, peers, finish, 0)
    own_sol.wait()


def owner_solve(rhs, lower, upper, pivot, peers, group=4):
    return pl.pallas_call(
        functools.partial(owner_kernel, peers, group),
        out_shape=jax.ShapeDtypeStruct(rhs.shape, rhs.dtype),
        in_specs=[pl.BlockSpec(memory_space=pl.ANY)] * 4,
        out_specs=pl.BlockSpec(memory_space=pl.ANY),
        scratch_shapes=[
            pltpu.VMEM(rhs.shape, jnp.float32),
            pltpu.VMEM(rhs.shape, jnp.float32),
            pltpu.VMEM(lower.shape, lower.dtype),
            pltpu.VMEM(upper.shape, upper.dtype),
            pltpu.VMEM(pivot.shape, pivot.dtype),
            pltpu.SemaphoreType.DMA((peers,)),
            pltpu.SemaphoreType.DMA((peers,)),
            pltpu.SemaphoreType.DMA((peers,)),
            pltpu.SemaphoreType.DMA((peers,)),
            pltpu.SemaphoreType.DMA((5,)),
        ],
        compiler_params=pltpu.CompilerParams(
            collective_id=0, has_side_effects=True, vmem_limit_bytes=48 * 1024 * 1024
        ),
    )(rhs, lower, upper, pivot)


def per_device(
    adjoint, source, step_size, lengths, line_owner, coupling, lower_coef, upper_coef, pivot_inverse
):
    fields, circ_cells, axial_cells, points = adjoint.shape
    line_count = circ_cells * axial_cells
    circ_devices = lax.axis_size("circ")
    capacity = 2 * line_count // circ_devices
    slot_count = lower_coef.shape[1]
    circ_padded = extended(adjoint, (("circ", 1),), 1, True)
    axial_padded = extended(adjoint, (("ax", 2),), 1, False)
    neighbours = (
        circ_padded[:, 2:],
        circ_padded[:, :-2],
        axial_padded[:, :, 2:],
        axial_padded[:, :, :-2],
    )
    coupled = None
    for k, near in enumerate(neighbours):
        for g in range(fields):
            term = coupling[k, :, g][:, None, None, None] * near[g][None]
            coupled = term if coupled is None else coupled + term
    residual = source - adjoint + step_size[None] * coupled
    active = jnp.arange(points)[None, None, None, :] < lengths[None, :, :, None]
    residual = jnp.where(active, residual, jnp.nan)
    line_rhs = residual.reshape(fields, line_count, points)
    targets = line_owner.reshape(line_count)
    ordinal = jnp.arange(line_count)
    earlier_same = (targets[:, None] == targets[None, :]) & (ordinal[None, :] < ordinal[:, None])
    slot_ids = targets * capacity + jnp.sum(earlier_same, axis=1)
    line_of_slot = jnp.full((slot_count,), line_count, jnp.int32).at[slot_ids].set(
        ordinal.astype(jnp.int32)
    )
    padded_rhs = jnp.concatenate(
        [line_rhs, jnp.full((fields, 1, points), jnp.nan, jnp.float32)], axis=1
    )
    outgoing = jnp.take(padded_rhs, line_of_slot, axis=1)
    returned = owner_solve(
        outgoing,
        lower_coef[0].transpose(1, 0, 2),
        upper_coef[0].transpose(1, 0, 2),
        pivot_inverse[0].transpose(1, 0, 2),
        circ_devices,
    )
    correction = jnp.take(returned, slot_ids, axis=1)
    return adjoint + correction.reshape(fields, circ_cells, axial_cells, points)


def solution(mesh):
    placed = (
        P(None, "circ", "ax", None),
        P(None, "circ", "ax", None),
        P("circ", "ax", None),
        P("circ", "ax"),
        P("ax", "circ", None, None),
        P(),
        P("ax", "circ", None, None),
        P("ax", "circ", None, None),
        P("ax", "circ", None, None),
    )
    return jax.shard_map(
        per_device,
        mesh=mesh,
        in_specs=placed,
        out_specs=P(None, "circ", "ax", None),
        check_vma=False,
    )
```

```python
import functools

import jax
import jax.numpy as jnp
from jax import lax
from jax.experimental import pallas as pl
from jax.experimental.pallas import tpu as pltpu
from jax.sharding import PartitionSpec as P


def extended(block, sides, width, periodic):
    for axis, dim in sides:
        count = lax.axis_size(axis)
        forward = [(i, i + 1) for i in range(count - 1)]
        if periodic:
            forward.append((count - 1, 0))
        backward = [(target, source) for source, target in forward]
        low = lax.ppermute(
            lax.slice_in_dim(block, block.shape[dim] - width, None, axis=dim), axis, forward
        )
        high = lax.ppermute(lax.slice_in_dim(block, 0, width, axis=dim), axis, backward)
        block = jnp.concatenate([low, block, high], axis=dim)
    return block


def scan_forward(coef, value, pos):
    points = value.shape[-1]
    shift = 1
    while shift < points:
        keep = pos >= shift
        value = value + coef * jnp.where(keep, pltpu.roll(value, shift, 2), 0.0)
        coef = coef * pltpu.roll(coef, shift, 2)
        shift *= 2
    return value


def scan_backward(coef, value, pos):
    points = value.shape[-1]
    shift = 1
    while shift < points:
        keep = pos < points - shift
        value = value + coef * jnp.where(keep, pltpu.roll(value, points - shift, 2), 0.0)
        coef = coef * pltpu.roll(coef, points - shift, 2)
        shift *= 2
    return value


MESH = pl.DeviceIdType.MESH


def exchange_kernel(peers, x_ref, o_ref, send_sems, recv_sems, local_sem):
    width = x_ref.shape[1] // peers
    me = lax.axis_index("circ")
    plane = lax.axis_index("ax")
    barrier = pltpu.get_barrier_semaphore()

    def greet(i, carry):
        peer = lax.rem(me + i, peers)
        pl.semaphore_signal(barrier, inc=1, device_id=(peer, plane), device_id_type=MESH)
        return carry

    lax.fori_loop(1, peers, greet, 0)
    pl.semaphore_wait(barrier, peers - 1)
    own = pl.ds(me * width, width)
    local = pltpu.make_async_copy(x_ref.at[:, own], o_ref.at[:, own], local_sem)
    local.start()

    def outgoing(i):
        peer = lax.rem(me + i, peers)
        return pltpu.make_async_remote_copy(
            src_ref=x_ref.at[:, pl.ds(peer * width, width)],
            dst_ref=o_ref.at[:, pl.ds(me * width, width)],
            send_sem=send_sems.at[peer],
            recv_sem=recv_sems.at[me],
            device_id=(peer, plane),
            device_id_type=MESH,
        )

    def incoming(i):
        peer = lax.rem(me + peers - i, peers)
        return pltpu.make_async_remote_copy(
            src_ref=x_ref.at[:, pl.ds(me * width, width)],
            dst_ref=o_ref.at[:, pl.ds(peer * width, width)],
            send_sem=send_sems.at[me],
            recv_sem=recv_sems.at[peer],
            device_id=(peer, plane),
            device_id_type=MESH,
        )

    def start(i, carry):
        outgoing(i).start()
        return carry

    def finish(i, carry):
        outgoing(i).wait_send()
        incoming(i).wait_recv()
        return carry

    lax.fori_loop(1, peers, start, 0)
    local.wait()
    lax.fori_loop(1, peers, finish, 0)


def exchange(chunks, peers, collective_id):
    return pl.pallas_call(
        functools.partial(exchange_kernel, peers),
        out_shape=jax.ShapeDtypeStruct(chunks.shape, chunks.dtype),
        in_specs=[pl.BlockSpec(memory_space=pl.ANY)],
        out_specs=pl.BlockSpec(memory_space=pl.ANY),
        scratch_shapes=[
            pltpu.SemaphoreType.DMA((peers,)),
            pltpu.SemaphoreType.DMA((peers,)),
            pltpu.SemaphoreType.DMA(()),
        ],
        compiler_params=pltpu.CompilerParams(collective_id=collective_id, has_side_effects=True),
    )(chunks)


def solve_rows(rhs, lower, upper, pivot):
    fields, rows, points = rhs.shape
    pos = lax.broadcasted_iota(jnp.int32, (fields, rows, points), 2)
    active = rhs == rhs
    forward_coef = jnp.where(active, -lower.astype(jnp.float32), 0.0)
    interim = scan_forward(forward_coef, jnp.where(active, rhs, 0.0), pos)
    applied = []
    for f in range(fields):
        total = pivot[f * fields].astype(jnp.float32) * interim[0]
        for g in range(1, fields):
            total = total + pivot[f * fields + g].astype(jnp.float32) * interim[g]
        applied.append(total)
    applied = jnp.stack(applied, axis=0)
    backward_coef = jnp.where(active, -upper.astype(jnp.float32), 0.0)
    return scan_backward(backward_coef, jnp.where(active, applied, 0.0), pos)


def owner_kernel(
    peers, group, rhs_ref, lower_ref, upper_ref, pivot_ref, out_ref,
    rhs_in, solved, lower_v, upper_v, pivot_v,
    send_rhs, recv_rhs, send_sol, recv_sol, local_sems,
):
    width = rhs_ref.shape[0] // peers
    fields, _, points = lower_ref.shape
    groups = peers // group
    rows = group * width
    me = lax.axis_index("circ")
    plane = lax.axis_index("ax")
    mine = me // group
    factor_copies = [
        pltpu.make_async_copy(lower_ref, lower_v, local_sems.at[0]),
        pltpu.make_async_copy(upper_ref, upper_v, local_sems.at[1]),
        pltpu.make_async_copy(pivot_ref, pivot_v, local_sems.at[2]),
    ]
    for copy in factor_copies:
        copy.start()
    barrier = pltpu.get_barrier_semaphore()

    def greet(i, carry):
        peer = lax.rem(me + i, peers)
        pl.semaphore_signal(barrier, inc=1, device_id=(peer, plane), device_id_type=MESH)
        return carry

    lax.fori_loop(1, peers, greet, 0)
    pl.semaphore_wait(barrier, peers - 1)

    def window(index):
        return pl.ds(index * width, width)

    def rhs_copy(source, target):
        return pltpu.make_async_remote_copy(
            src_ref=rhs_ref.at[window(target)],
            dst_ref=rhs_in.at[window(source)],
            send_sem=send_rhs.at[target],
            recv_sem=recv_rhs.at[source],
            device_id=(lax.select(source == me, target, source), plane),
            device_id_type=MESH,
        )

    def sol_copy(source, target):
        return pltpu.make_async_remote_copy(
            src_ref=solved.at[window(target)],
            dst_ref=out_ref.at[window(source)],
            send_sem=send_sol.at[target],
            recv_sem=recv_sol.at[source],
            device_id=(lax.select(source == me, target, source), plane),
            device_id_type=MESH,
        )

    own_rhs = pltpu.make_async_copy(rhs_ref.at[window(me)], rhs_in.at[window(me)], local_sems.at[3])
    own_sol = pltpu.make_async_copy(solved.at[window(me)], out_ref.at[window(me)], local_sems.at[4])

    def send(i, carry):
        target = group * lax.rem(mine - i // group + groups, groups) + i % group

        @pl.when(target == me)
        def _():
            own_rhs.start()

        @pl.when(target != me)
        def _():
            rhs_copy(me, target).start()

        return carry

    lax.fori_loop(0, peers, send, 0)
    for copy in factor_copies:
        copy.wait()

    def solve(j, carry):
        g = lax.rem(mine + j, groups)
        for r in range(group):
            source = g * group + r

            @pl.when(source == me)
            def _():
                own_rhs.wait()

            @pl.when(source != me)
            def _():
                rhs_copy(source, me).wait_recv()

        block = pl.ds(pl.multiple_of(g * rows, rows), rows)
        by_field = [pl.ds(f * points, points) for f in range(fields)]
        rhs = jnp.stack([rhs_in[block, lanes] for lanes in by_field], axis=0)
        result = solve_rows(rhs, lower_v[:, block, :], upper_v[:, block, :], pivot_v[:, block, :])
        for f, lanes in enumerate(by_field):
            solved[block, lanes] = result[f]
        for r in range(group):
            target = g * group + r

            @pl.when(target == me)
            def _():
                own_sol.start()

            @pl.when(target != me)
            def _():
                sol_copy(me, target).start()

        return carry

    lax.fori_loop(0, groups, solve, 0)

    def finish(i, carry):
        peer = lax.rem(me + i, peers)
        rhs_copy(me, peer).wait_send()
        sol_copy(me, peer).wait_send()
        sol_copy(peer, me).wait_recv()
        return carry

    lax.fori_loop(1, peers, finish, 0)
    own_sol.wait()


def owner_solve(rhs, lower, upper, pivot, peers, group=4):
    return pl.pallas_call(
        functools.partial(owner_kernel, peers, group),
        out_shape=jax.ShapeDtypeStruct(rhs.shape, rhs.dtype),
        in_specs=[pl.BlockSpec(memory_space=pl.ANY)] * 4,
        out_specs=pl.BlockSpec(memory_space=pl.ANY),
        scratch_shapes=[
            pltpu.VMEM(rhs.shape, jnp.float32),
            pltpu.VMEM(rhs.shape, jnp.float32),
            pltpu.VMEM(lower.shape, lower.dtype),
            pltpu.VMEM(upper.shape, upper.dtype),
            pltpu.VMEM(pivot.shape, pivot.dtype),
            pltpu.SemaphoreType.DMA((peers,)),
            pltpu.SemaphoreType.DMA((peers,)),
            pltpu.SemaphoreType.DMA((peers,)),
            pltpu.SemaphoreType.DMA((peers,)),
            pltpu.SemaphoreType.DMA((5,)),
        ],
        compiler_params=pltpu.CompilerParams(
            collective_id=0, has_side_effects=True, vmem_limit_bytes=48 * 1024 * 1024
        ),
    )(rhs, lower, upper, pivot)


def per_device(
    adjoint, source, step_size, lengths, line_owner, coupling, lower_coef, upper_coef, pivot_inverse
):
    fields, circ_cells, axial_cells, points = adjoint.shape
    line_count = circ_cells * axial_cells
    circ_devices = lax.axis_size("circ")
    capacity = 2 * line_count // circ_devices
    slot_count = lower_coef.shape[1]
    circ_padded = extended(adjoint, (("circ", 1),), 1, True)
    axial_padded = extended(adjoint, (("ax", 2),), 1, False)
    neighbours = (
        circ_padded[:, 2:],
        circ_padded[:, :-2],
        axial_padded[:, :, 2:],
        axial_padded[:, :, :-2],
    )
    coupled = None
    for k, near in enumerate(neighbours):
        for g in range(fields):
            term = coupling[k, :, g][:, None, None, None] * near[g][None]
            coupled = term if coupled is None else coupled + term
    residual = source - adjoint + step_size[None] * coupled
    active = jnp.arange(points)[None, None, None, :] < lengths[None, :, :, None]
    residual = jnp.where(active, residual, jnp.nan)
    line_rhs = residual.transpose(1, 2, 0, 3).reshape(line_count, fields * points)
    targets = line_owner.reshape(line_count)
    ordinal = jnp.arange(line_count)
    earlier_same = (targets[:, None] == targets[None, :]) & (ordinal[None, :] < ordinal[:, None])
    slot_ids = targets * capacity + jnp.sum(earlier_same, axis=1)
    line_of_slot = jnp.full((slot_count,), line_count, jnp.int32).at[slot_ids].set(
        ordinal.astype(jnp.int32)
    )
    padded_rhs = jnp.concatenate(
        [line_rhs, jnp.full((1, fields * points), jnp.nan, jnp.float32)], axis=0
    )
    outgoing = jnp.take(padded_rhs, line_of_slot, axis=0)
    returned = owner_solve(
        outgoing,
        lower_coef[0].transpose(1, 0, 2),
        upper_coef[0].transpose(1, 0, 2),
        pivot_inverse[0].transpose(1, 0, 2),
        circ_devices,
    )
    correction = jnp.take(returned, slot_ids, axis=0)
    correction = correction.reshape(circ_cells, axial_cells, fields, points).transpose(2, 0, 1, 3)
    return adjoint + correction


def solution(mesh):
    placed = (
        P(None, "circ", "ax", None),
        P(None, "circ", "ax", None),
        P("circ", "ax", None),
        P("circ", "ax"),
        P("ax", "circ", None, None),
        P(),
        P("ax", "circ", None, None),
        P("ax", "circ", None, None),
        P("ax", "circ", None, None),
    )
    return jax.shard_map(
        per_device,
        mesh=mesh,
        in_specs=placed,
        out_specs=P(None, "circ", "ax", None),
        check_vma=False,
    )
```

```python
import functools

import jax
import jax.numpy as jnp
from jax import lax
from jax.experimental import pallas as pl
from jax.experimental.pallas import tpu as pltpu
from jax.sharding import PartitionSpec as P


def extended(block, sides, width, periodic):
    for axis, dim in sides:
        count = lax.axis_size(axis)
        forward = [(i, i + 1) for i in range(count - 1)]
        if periodic:
            forward.append((count - 1, 0))
        backward = [(target, source) for source, target in forward]
        low = lax.ppermute(
            lax.slice_in_dim(block, block.shape[dim] - width, None, axis=dim), axis, forward
        )
        high = lax.ppermute(lax.slice_in_dim(block, 0, width, axis=dim), axis, backward)
        block = jnp.concatenate([low, block, high], axis=dim)
    return block


def scan_forward(coef, value, pos):
    points = value.shape[-1]
    shift = 1
    while shift < points:
        keep = pos >= shift
        value = value + coef * jnp.where(keep, pltpu.roll(value, shift, 2), 0.0)
        coef = coef * pltpu.roll(coef, shift, 2)
        shift *= 2
    return value


def scan_backward(coef, value, pos):
    points = value.shape[-1]
    shift = 1
    while shift < points:
        keep = pos < points - shift
        value = value + coef * jnp.where(keep, pltpu.roll(value, points - shift, 2), 0.0)
        coef = coef * pltpu.roll(coef, points - shift, 2)
        shift *= 2
    return value


MESH = pl.DeviceIdType.MESH


def solve_rows(rhs, lower, upper, pivot):
    fields, rows, points = rhs.shape
    pos = lax.broadcasted_iota(jnp.int32, (fields, rows, points), 2)
    active = rhs == rhs
    forward_coef = jnp.where(active, -lower.astype(jnp.float32), 0.0)
    interim = scan_forward(forward_coef, jnp.where(active, rhs, 0.0), pos)
    applied = []
    for f in range(fields):
        total = pivot[f * fields].astype(jnp.float32) * interim[0]
        for g in range(1, fields):
            total = total + pivot[f * fields + g].astype(jnp.float32) * interim[g]
        applied.append(total)
    applied = jnp.stack(applied, axis=0)
    backward_coef = jnp.where(active, -upper.astype(jnp.float32), 0.0)
    return scan_backward(backward_coef, jnp.where(active, applied, 0.0), pos)


def owner_kernel(
    peers, group, ahead, rhs_ref, lower_ref, upper_ref, pivot_ref, out_ref,
    rhs_in, solved, lower_v, upper_v, pivot_v,
    send_rhs, recv_rhs, send_sol, recv_sol, local_sems,
):
    width = rhs_ref.shape[0] // peers
    fields, _, points = lower_ref.shape
    groups = peers // group
    rows = group * width
    me = lax.axis_index("circ")
    plane = lax.axis_index("ax")
    mine = me // group
    factor_copies = [
        pltpu.make_async_copy(lower_ref, lower_v, local_sems.at[0]),
        pltpu.make_async_copy(upper_ref, upper_v, local_sems.at[1]),
        pltpu.make_async_copy(pivot_ref, pivot_v, local_sems.at[2]),
    ]
    for copy in factor_copies:
        copy.start()
    barrier = pltpu.get_barrier_semaphore()

    def greet(i, carry):
        peer = lax.rem(me + i, peers)
        pl.semaphore_signal(barrier, inc=1, device_id=(peer, plane), device_id_type=MESH)
        return carry

    lax.fori_loop(1, peers, greet, 0)
    pl.semaphore_wait(barrier, peers - 1)

    def window(index):
        return pl.ds(index * width, width)

    def rhs_copy(source, target):
        return pltpu.make_async_remote_copy(
            src_ref=rhs_ref.at[window(target)],
            dst_ref=rhs_in.at[window(source)],
            send_sem=send_rhs.at[target],
            recv_sem=recv_rhs.at[source],
            device_id=(lax.select(source == me, target, source), plane),
            device_id_type=MESH,
        )

    def sol_copy(source, target):
        return pltpu.make_async_remote_copy(
            src_ref=solved.at[window(target)],
            dst_ref=out_ref.at[window(source)],
            send_sem=send_sol.at[target],
            recv_sem=recv_sol.at[source],
            device_id=(lax.select(source == me, target, source), plane),
            device_id_type=MESH,
        )

    own_rhs = pltpu.make_async_copy(rhs_ref.at[window(me)], rhs_in.at[window(me)], local_sems.at[3])
    own_sol = pltpu.make_async_copy(solved.at[window(me)], out_ref.at[window(me)], local_sems.at[4])

    def target_of(step, r):
        return group * lax.rem(mine - step + groups, groups) + r

    def send_step(step):
        for r in range(group):
            target = target_of(step, r)

            @pl.when(target == me)
            def _():
                own_rhs.start()

            @pl.when(target != me)
            def _():
                rhs_copy(me, target).start()

    def sent_step(step):
        for r in range(group):
            target = target_of(step, r)

            @pl.when(target != me)
            def _():
                rhs_copy(me, target).wait_send()

    for step in range(min(ahead, groups)):
        send_step(step)
    for copy in factor_copies:
        copy.wait()

    def solve(j, carry):
        @pl.when(j + ahead < groups)
        def _():
            sent_step(j)
            send_step(j + ahead)

        g = lax.rem(mine + j, groups)
        for r in range(group):
            source = g * group + r

            @pl.when(source == me)
            def _():
                own_rhs.wait()

            @pl.when(source != me)
            def _():
                rhs_copy(source, me).wait_recv()

        block = pl.ds(pl.multiple_of(g * rows, rows), rows)
        by_field = [pl.ds(f * points, points) for f in range(fields)]
        rhs = jnp.stack([rhs_in[block, lanes] for lanes in by_field], axis=0)
        result = solve_rows(rhs, lower_v[:, block, :], upper_v[:, block, :], pivot_v[:, block, :])
        for f, lanes in enumerate(by_field):
            solved[block, lanes] = result[f]
        for r in range(group):
            target = g * group + r

            @pl.when(target == me)
            def _():
                own_sol.start()

            @pl.when(target != me)
            def _():
                sol_copy(me, target).start()

        return carry

    lax.fori_loop(0, groups, solve, 0)
    for step in range(max(groups - ahead, 0), groups):
        sent_step(step)

    def finish(i, carry):
        peer = lax.rem(me + i, peers)
        sol_copy(me, peer).wait_send()
        sol_copy(peer, me).wait_recv()
        return carry

    lax.fori_loop(1, peers, finish, 0)
    own_sol.wait()


def owner_solve(rhs, lower, upper, pivot, peers, group=4, ahead=3):
    return pl.pallas_call(
        functools.partial(owner_kernel, peers, group, ahead),
        out_shape=jax.ShapeDtypeStruct(rhs.shape, rhs.dtype),
        in_specs=[pl.BlockSpec(memory_space=pl.ANY)] * 4,
        out_specs=pl.BlockSpec(memory_space=pl.ANY),
        scratch_shapes=[
            pltpu.VMEM(rhs.shape, jnp.float32),
            pltpu.VMEM(rhs.shape, jnp.float32),
            pltpu.VMEM(lower.shape, lower.dtype),
            pltpu.VMEM(upper.shape, upper.dtype),
            pltpu.VMEM(pivot.shape, pivot.dtype),
            pltpu.SemaphoreType.DMA((peers,)),
            pltpu.SemaphoreType.DMA((peers,)),
            pltpu.SemaphoreType.DMA((peers,)),
            pltpu.SemaphoreType.DMA((peers,)),
            pltpu.SemaphoreType.DMA((5,)),
        ],
        compiler_params=pltpu.CompilerParams(
            collective_id=0, has_side_effects=True, vmem_limit_bytes=48 * 1024 * 1024
        ),
    )(rhs, lower, upper, pivot)


def per_device(
    adjoint, source, step_size, lengths, line_owner, coupling, lower_coef, upper_coef, pivot_inverse
):
    fields, circ_cells, axial_cells, points = adjoint.shape
    line_count = circ_cells * axial_cells
    circ_devices = lax.axis_size("circ")
    capacity = 2 * line_count // circ_devices
    slot_count = lower_coef.shape[1]
    circ_padded = extended(adjoint, (("circ", 1),), 1, True)
    axial_padded = extended(adjoint, (("ax", 2),), 1, False)
    neighbours = (
        circ_padded[:, 2:],
        circ_padded[:, :-2],
        axial_padded[:, :, 2:],
        axial_padded[:, :, :-2],
    )
    coupled = None
    for k, near in enumerate(neighbours):
        for g in range(fields):
            term = coupling[k, :, g][:, None, None, None] * near[g][None]
            coupled = term if coupled is None else coupled + term
    residual = source - adjoint + step_size[None] * coupled
    active = jnp.arange(points)[None, None, None, :] < lengths[None, :, :, None]
    residual = jnp.where(active, residual, jnp.nan)
    line_rhs = residual.transpose(1, 2, 0, 3).reshape(line_count, fields * points)
    targets = line_owner.reshape(line_count)
    ordinal = jnp.arange(line_count)
    earlier_same = (targets[:, None] == targets[None, :]) & (ordinal[None, :] < ordinal[:, None])
    slot_ids = targets * capacity + jnp.sum(earlier_same, axis=1)
    line_of_slot = jnp.full((slot_count,), line_count, jnp.int32).at[slot_ids].set(
        ordinal.astype(jnp.int32)
    )
    padded_rhs = jnp.concatenate(
        [line_rhs, jnp.full((1, fields * points), jnp.nan, jnp.float32)], axis=0
    )
    outgoing = jnp.take(padded_rhs, line_of_slot, axis=0)
    returned = owner_solve(
        outgoing,
        lower_coef[0].transpose(1, 0, 2),
        upper_coef[0].transpose(1, 0, 2),
        pivot_inverse[0].transpose(1, 0, 2),
        circ_devices,
    )
    correction = jnp.take(returned, slot_ids, axis=0)
    correction = correction.reshape(circ_cells, axial_cells, fields, points).transpose(2, 0, 1, 3)
    return adjoint + correction


def solution(mesh):
    placed = (
        P(None, "circ", "ax", None),
        P(None, "circ", "ax", None),
        P("circ", "ax", None),
        P("circ", "ax"),
        P("ax", "circ", None, None),
        P(),
        P("ax", "circ", None, None),
        P("ax", "circ", None, None),
        P("ax", "circ", None, None),
    )
    return jax.shard_map(
        per_device,
        mesh=mesh,
        in_specs=placed,
        out_specs=P(None, "circ", "ax", None),
        check_vma=False,
    )
```

```python
import functools

import jax
import jax.numpy as jnp
from jax import lax
from jax.experimental import pallas as pl
from jax.experimental.pallas import tpu as pltpu
from jax.sharding import PartitionSpec as P


def extended(block, sides, width, periodic):
    for axis, dim in sides:
        count = lax.axis_size(axis)
        forward = [(i, i + 1) for i in range(count - 1)]
        if periodic:
            forward.append((count - 1, 0))
        backward = [(target, source) for source, target in forward]
        low = lax.ppermute(
            lax.slice_in_dim(block, block.shape[dim] - width, None, axis=dim), axis, forward
        )
        high = lax.ppermute(lax.slice_in_dim(block, 0, width, axis=dim), axis, backward)
        block = jnp.concatenate([low, block, high], axis=dim)
    return block


def scan_forward(coef, value, pos):
    points = value.shape[-1]
    shift = 1
    while shift < points:
        keep = pos >= shift
        value = value + coef * jnp.where(keep, pltpu.roll(value, shift, 2), 0.0)
        coef = coef * pltpu.roll(coef, shift, 2)
        shift *= 2
    return value


def scan_backward(coef, value, pos):
    points = value.shape[-1]
    shift = 1
    while shift < points:
        keep = pos < points - shift
        value = value + coef * jnp.where(keep, pltpu.roll(value, points - shift, 2), 0.0)
        coef = coef * pltpu.roll(coef, points - shift, 2)
        shift *= 2
    return value


MESH = pl.DeviceIdType.MESH


def solve_rows(rhs, lower, upper, pivot):
    fields, rows, points = rhs.shape
    pos = lax.broadcasted_iota(jnp.int32, (fields, rows, points), 2)
    active = rhs == rhs
    forward_coef = jnp.where(active, -lower.astype(jnp.float32), 0.0)
    interim = scan_forward(forward_coef, jnp.where(active, rhs, 0.0), pos)
    applied = []
    for f in range(fields):
        total = pivot[f * fields].astype(jnp.float32) * interim[0]
        for g in range(1, fields):
            total = total + pivot[f * fields + g].astype(jnp.float32) * interim[g]
        applied.append(total)
    applied = jnp.stack(applied, axis=0)
    backward_coef = jnp.where(active, -upper.astype(jnp.float32), 0.0)
    return scan_backward(backward_coef, jnp.where(active, applied, 0.0), pos)


def owner_kernel(
    peers, group, rhs_ref, lower_ref, upper_ref, pivot_ref, out_ref,
    rhs_in, solved, lower_v, upper_v, pivot_v,
    send_rhs, recv_rhs, send_sol, recv_sol, local_sems,
):
    width = rhs_ref.shape[0] // peers
    fields, _, points = lower_ref.shape
    groups = peers // group
    rows = group * width
    me = lax.axis_index("circ")
    plane = lax.axis_index("ax")
    mine = me // group
    factor_copies = [
        pltpu.make_async_copy(lower_ref, lower_v, local_sems.at[0]),
        pltpu.make_async_copy(upper_ref, upper_v, local_sems.at[1]),
        pltpu.make_async_copy(pivot_ref, pivot_v, local_sems.at[2]),
    ]
    for copy in factor_copies:
        copy.start()
    barrier = pltpu.get_barrier_semaphore()

    def greet(i, carry):
        peer = lax.rem(me + i, peers)
        pl.semaphore_signal(barrier, inc=1, device_id=(peer, plane), device_id_type=MESH)
        return carry

    lax.fori_loop(1, peers, greet, 0)
    pl.semaphore_wait(barrier, peers - 1)

    def window(index):
        return pl.ds(index * width, width)

    def rhs_copy(source, target):
        return pltpu.make_async_remote_copy(
            src_ref=rhs_ref.at[window(target)],
            dst_ref=rhs_in.at[window(source)],
            send_sem=send_rhs.at[target],
            recv_sem=recv_rhs.at[source],
            device_id=(lax.select(source == me, target, source), plane),
            device_id_type=MESH,
        )

    def sol_copy(source, target):
        return pltpu.make_async_remote_copy(
            src_ref=solved.at[window(target)],
            dst_ref=out_ref.at[window(source)],
            send_sem=send_sol.at[target],
            recv_sem=recv_sol.at[source],
            device_id=(lax.select(source == me, target, source), plane),
            device_id_type=MESH,
        )

    own_rhs = pltpu.make_async_copy(rhs_ref.at[window(me)], rhs_in.at[window(me)], local_sems.at[3])
    own_sol = pltpu.make_async_copy(solved.at[window(me)], out_ref.at[window(me)], local_sems.at[4])

    def order(step):
        half = step // 2
        return lax.select(step % 2 == 0, half, groups - 1 - half)

    def send(i, carry):
        target = group * lax.rem(mine - order(i // group) + groups, groups) + i % group

        @pl.when(target == me)
        def _():
            own_rhs.start()

        @pl.when(target != me)
        def _():
            rhs_copy(me, target).start()

        return carry

    lax.fori_loop(0, peers, send, 0)
    for copy in factor_copies:
        copy.wait()

    def solve(j, carry):
        g = lax.rem(mine + order(j), groups)
        for r in range(group):
            source = g * group + r

            @pl.when(source == me)
            def _():
                own_rhs.wait()

            @pl.when(source != me)
            def _():
                rhs_copy(source, me).wait_recv()

        block = pl.ds(pl.multiple_of(g * rows, rows), rows)
        by_field = [pl.ds(f * points, points) for f in range(fields)]
        rhs = jnp.stack([rhs_in[block, lanes] for lanes in by_field], axis=0)
        result = solve_rows(rhs, lower_v[:, block, :], upper_v[:, block, :], pivot_v[:, block, :])
        for f, lanes in enumerate(by_field):
            solved[block, lanes] = result[f]
        for r in range(group):
            target = g * group + r

            @pl.when(target == me)
            def _():
                own_sol.start()

            @pl.when(target != me)
            def _():
                sol_copy(me, target).start()

        return carry

    lax.fori_loop(0, groups, solve, 0)

    def finish(i, carry):
        peer = lax.rem(me + i, peers)
        rhs_copy(me, peer).wait_send()
        sol_copy(me, peer).wait_send()
        sol_copy(peer, me).wait_recv()
        return carry

    lax.fori_loop(1, peers, finish, 0)
    own_sol.wait()


def owner_solve(rhs, lower, upper, pivot, peers, group=4):
    return pl.pallas_call(
        functools.partial(owner_kernel, peers, group),
        out_shape=jax.ShapeDtypeStruct(rhs.shape, rhs.dtype),
        in_specs=[pl.BlockSpec(memory_space=pl.ANY)] * 4,
        out_specs=pl.BlockSpec(memory_space=pl.ANY),
        scratch_shapes=[
            pltpu.VMEM(rhs.shape, jnp.float32),
            pltpu.VMEM(rhs.shape, jnp.float32),
            pltpu.VMEM(lower.shape, lower.dtype),
            pltpu.VMEM(upper.shape, upper.dtype),
            pltpu.VMEM(pivot.shape, pivot.dtype),
            pltpu.SemaphoreType.DMA((peers,)),
            pltpu.SemaphoreType.DMA((peers,)),
            pltpu.SemaphoreType.DMA((peers,)),
            pltpu.SemaphoreType.DMA((peers,)),
            pltpu.SemaphoreType.DMA((5,)),
        ],
        compiler_params=pltpu.CompilerParams(
            collective_id=0, has_side_effects=True, vmem_limit_bytes=48 * 1024 * 1024
        ),
    )(rhs, lower, upper, pivot)


def per_device(
    adjoint, source, step_size, lengths, line_owner, coupling, lower_coef, upper_coef, pivot_inverse
):
    fields, circ_cells, axial_cells, points = adjoint.shape
    line_count = circ_cells * axial_cells
    circ_devices = lax.axis_size("circ")
    capacity = 2 * line_count // circ_devices
    slot_count = lower_coef.shape[1]
    circ_padded = extended(adjoint, (("circ", 1),), 1, True)
    axial_padded = extended(adjoint, (("ax", 2),), 1, False)
    neighbours = (
        circ_padded[:, 2:],
        circ_padded[:, :-2],
        axial_padded[:, :, 2:],
        axial_padded[:, :, :-2],
    )
    coupled = None
    for k, near in enumerate(neighbours):
        for g in range(fields):
            term = coupling[k, :, g][:, None, None, None] * near[g][None]
            coupled = term if coupled is None else coupled + term
    residual = source - adjoint + step_size[None] * coupled
    active = jnp.arange(points)[None, None, None, :] < lengths[None, :, :, None]
    residual = jnp.where(active, residual, jnp.nan)
    line_rhs = residual.transpose(1, 2, 0, 3).reshape(line_count, fields * points)
    targets = line_owner.reshape(line_count)
    ordinal = jnp.arange(line_count)
    earlier_same = (targets[:, None] == targets[None, :]) & (ordinal[None, :] < ordinal[:, None])
    slot_ids = targets * capacity + jnp.sum(earlier_same, axis=1)
    line_of_slot = jnp.full((slot_count,), line_count, jnp.int32).at[slot_ids].set(
        ordinal.astype(jnp.int32)
    )
    padded_rhs = jnp.concatenate(
        [line_rhs, jnp.full((1, fields * points), jnp.nan, jnp.float32)], axis=0
    )
    outgoing = jnp.take(padded_rhs, line_of_slot, axis=0)
    returned = owner_solve(
        outgoing,
        lower_coef[0].transpose(1, 0, 2),
        upper_coef[0].transpose(1, 0, 2),
        pivot_inverse[0].transpose(1, 0, 2),
        circ_devices,
    )
    correction = jnp.take(returned, slot_ids, axis=0)
    correction = correction.reshape(circ_cells, axial_cells, fields, points).transpose(2, 0, 1, 3)
    return adjoint + correction


def solution(mesh):
    placed = (
        P(None, "circ", "ax", None),
        P(None, "circ", "ax", None),
        P("circ", "ax", None),
        P("circ", "ax"),
        P("ax", "circ", None, None),
        P(),
        P("ax", "circ", None, None),
        P("ax", "circ", None, None),
        P("ax", "circ", None, None),
    )
    return jax.shard_map(
        per_device,
        mesh=mesh,
        in_specs=placed,
        out_specs=P(None, "circ", "ax", None),
        check_vma=False,
    )
```

```python
import functools

import jax
import jax.numpy as jnp
from jax import lax
from jax.experimental import pallas as pl
from jax.experimental.pallas import tpu as pltpu
from jax.sharding import PartitionSpec as P


def extended(block, sides, width, periodic):
    for axis, dim in sides:
        count = lax.axis_size(axis)
        forward = [(i, i + 1) for i in range(count - 1)]
        if periodic:
            forward.append((count - 1, 0))
        backward = [(target, source) for source, target in forward]
        low = lax.ppermute(
            lax.slice_in_dim(block, block.shape[dim] - width, None, axis=dim), axis, forward
        )
        high = lax.ppermute(lax.slice_in_dim(block, 0, width, axis=dim), axis, backward)
        block = jnp.concatenate([low, block, high], axis=dim)
    return block


def scan_forward(coef, value, pos):
    points = value.shape[-1]
    shift = 1
    while shift < points:
        keep = pos >= shift
        value = value + coef * jnp.where(keep, pltpu.roll(value, shift, 2), 0.0)
        coef = coef * pltpu.roll(coef, shift, 2)
        shift *= 2
    return value


def scan_backward(coef, value, pos):
    points = value.shape[-1]
    shift = 1
    while shift < points:
        keep = pos < points - shift
        value = value + coef * jnp.where(keep, pltpu.roll(value, points - shift, 2), 0.0)
        coef = coef * pltpu.roll(coef, points - shift, 2)
        shift *= 2
    return value


MESH = pl.DeviceIdType.MESH


def solve_rows(rhs, lower, upper, pivot):
    fields, rows, points = rhs.shape
    pos = lax.broadcasted_iota(jnp.int32, (fields, rows, points), 2)
    active = rhs == rhs
    forward_coef = jnp.where(active, -lower.astype(jnp.float32), 0.0)
    interim = scan_forward(forward_coef, jnp.where(active, rhs, 0.0), pos)
    applied = []
    for f in range(fields):
        total = pivot[f * fields].astype(jnp.float32) * interim[0]
        for g in range(1, fields):
            total = total + pivot[f * fields + g].astype(jnp.float32) * interim[g]
        applied.append(total)
    applied = jnp.stack(applied, axis=0)
    backward_coef = jnp.where(active, -upper.astype(jnp.float32), 0.0)
    return scan_backward(backward_coef, jnp.where(active, applied, 0.0), pos)


def owner_kernel(
    peers, group, rhs_ref, lower_ref, upper_ref, pivot_ref, out_ref,
    rhs_in, solved, lower_v, upper_v, pivot_v,
    send_rhs, recv_rhs, send_sol, recv_sol, local_sems,
):
    width = rhs_ref.shape[0] // peers
    fields, _, points = lower_ref.shape
    groups = peers // group
    rows = group * width
    me = lax.axis_index("circ")
    plane = lax.axis_index("ax")
    mine = me // group
    factor_copies = [
        pltpu.make_async_copy(lower_ref, lower_v, local_sems.at[0]),
        pltpu.make_async_copy(upper_ref, upper_v, local_sems.at[1]),
        pltpu.make_async_copy(pivot_ref, pivot_v, local_sems.at[2]),
    ]
    for copy in factor_copies:
        copy.start()
    barrier = pltpu.get_barrier_semaphore()

    def greet(i, carry):
        peer = lax.rem(me + i, peers)
        pl.semaphore_signal(barrier, inc=1, device_id=(peer, plane), device_id_type=MESH)
        return carry

    lax.fori_loop(1, peers, greet, 0)
    pl.semaphore_wait(barrier, peers - 1)

    def window(index):
        return pl.ds(index * width, width)

    def rhs_copy(source, target):
        return pltpu.make_async_remote_copy(
            src_ref=rhs_ref.at[window(target)],
            dst_ref=rhs_in.at[window(source)],
            send_sem=send_rhs.at[target],
            recv_sem=recv_rhs.at[source],
            device_id=(lax.select(source == me, target, source), plane),
            device_id_type=MESH,
        )

    def sol_copy(source, target):
        return pltpu.make_async_remote_copy(
            src_ref=solved.at[window(target)],
            dst_ref=out_ref.at[window(source)],
            send_sem=send_sol.at[target],
            recv_sem=recv_sol.at[source],
            device_id=(lax.select(source == me, target, source), plane),
            device_id_type=MESH,
        )

    own_rhs = pltpu.make_async_copy(rhs_ref.at[window(me)], rhs_in.at[window(me)], local_sems.at[3])
    own_sol = pltpu.make_async_copy(solved.at[window(me)], out_ref.at[window(me)], local_sems.at[4])

    def order(step):
        quarter, kind = step // 4, step % 4
        near = lax.select(kind == 0, quarter, groups - 1 - quarter)
        far = lax.select(kind == 2, groups // 4 + quarter, 3 * groups // 4 - 1 - quarter)
        return lax.select(kind < 2, near, far)

    def send(i, carry):
        target = group * lax.rem(mine - order(i // group) + groups, groups) + i % group

        @pl.when(target == me)
        def _():
            own_rhs.start()

        @pl.when(target != me)
        def _():
            rhs_copy(me, target).start()

        return carry

    lax.fori_loop(0, peers, send, 0)
    for copy in factor_copies:
        copy.wait()

    def solve(j, carry):
        g = lax.rem(mine + order(j), groups)
        for r in range(group):
            source = g * group + r

            @pl.when(source == me)
            def _():
                own_rhs.wait()

            @pl.when(source != me)
            def _():
                rhs_copy(source, me).wait_recv()

        block = pl.ds(pl.multiple_of(g * rows, rows), rows)
        by_field = [pl.ds(f * points, points) for f in range(fields)]
        rhs = jnp.stack([rhs_in[block, lanes] for lanes in by_field], axis=0)
        result = solve_rows(rhs, lower_v[:, block, :], upper_v[:, block, :], pivot_v[:, block, :])
        for f, lanes in enumerate(by_field):
            solved[block, lanes] = result[f]
        for r in range(group):
            target = g * group + r

            @pl.when(target == me)
            def _():
                own_sol.start()

            @pl.when(target != me)
            def _():
                sol_copy(me, target).start()

        return carry

    lax.fori_loop(0, groups, solve, 0)

    def finish(i, carry):
        peer = lax.rem(me + i, peers)
        rhs_copy(me, peer).wait_send()
        sol_copy(me, peer).wait_send()
        sol_copy(peer, me).wait_recv()
        return carry

    lax.fori_loop(1, peers, finish, 0)
    own_sol.wait()


def owner_solve(rhs, lower, upper, pivot, peers, group=4):
    return pl.pallas_call(
        functools.partial(owner_kernel, peers, group),
        out_shape=jax.ShapeDtypeStruct(rhs.shape, rhs.dtype),
        in_specs=[pl.BlockSpec(memory_space=pl.ANY)] * 4,
        out_specs=pl.BlockSpec(memory_space=pl.ANY),
        scratch_shapes=[
            pltpu.VMEM(rhs.shape, jnp.float32),
            pltpu.VMEM(rhs.shape, jnp.float32),
            pltpu.VMEM(lower.shape, lower.dtype),
            pltpu.VMEM(upper.shape, upper.dtype),
            pltpu.VMEM(pivot.shape, pivot.dtype),
            pltpu.SemaphoreType.DMA((peers,)),
            pltpu.SemaphoreType.DMA((peers,)),
            pltpu.SemaphoreType.DMA((peers,)),
            pltpu.SemaphoreType.DMA((peers,)),
            pltpu.SemaphoreType.DMA((5,)),
        ],
        compiler_params=pltpu.CompilerParams(
            collective_id=0, has_side_effects=True, vmem_limit_bytes=48 * 1024 * 1024
        ),
    )(rhs, lower, upper, pivot)


def per_device(
    adjoint, source, step_size, lengths, line_owner, coupling, lower_coef, upper_coef, pivot_inverse
):
    fields, circ_cells, axial_cells, points = adjoint.shape
    line_count = circ_cells * axial_cells
    circ_devices = lax.axis_size("circ")
    capacity = 2 * line_count // circ_devices
    slot_count = lower_coef.shape[1]
    circ_padded = extended(adjoint, (("circ", 1),), 1, True)
    axial_padded = extended(adjoint, (("ax", 2),), 1, False)
    neighbours = (
        circ_padded[:, 2:],
        circ_padded[:, :-2],
        axial_padded[:, :, 2:],
        axial_padded[:, :, :-2],
    )
    coupled = None
    for k, near in enumerate(neighbours):
        for g in range(fields):
            term = coupling[k, :, g][:, None, None, None] * near[g][None]
            coupled = term if coupled is None else coupled + term
    residual = source - adjoint + step_size[None] * coupled
    active = jnp.arange(points)[None, None, None, :] < lengths[None, :, :, None]
    residual = jnp.where(active, residual, jnp.nan)
    line_rhs = residual.transpose(1, 2, 0, 3).reshape(line_count, fields * points)
    targets = line_owner.reshape(line_count)
    ordinal = jnp.arange(line_count)
    earlier_same = (targets[:, None] == targets[None, :]) & (ordinal[None, :] < ordinal[:, None])
    slot_ids = targets * capacity + jnp.sum(earlier_same, axis=1)
    line_of_slot = jnp.full((slot_count,), line_count, jnp.int32).at[slot_ids].set(
        ordinal.astype(jnp.int32)
    )
    padded_rhs = jnp.concatenate(
        [line_rhs, jnp.full((1, fields * points), jnp.nan, jnp.float32)], axis=0
    )
    outgoing = jnp.take(padded_rhs, line_of_slot, axis=0)
    returned = owner_solve(
        outgoing,
        lower_coef[0].transpose(1, 0, 2),
        upper_coef[0].transpose(1, 0, 2),
        pivot_inverse[0].transpose(1, 0, 2),
        circ_devices,
    )
    correction = jnp.take(returned, slot_ids, axis=0)
    correction = correction.reshape(circ_cells, axial_cells, fields, points).transpose(2, 0, 1, 3)
    return adjoint + correction


def solution(mesh):
    placed = (
        P(None, "circ", "ax", None),
        P(None, "circ", "ax", None),
        P("circ", "ax", None),
        P("circ", "ax"),
        P("ax", "circ", None, None),
        P(),
        P("ax", "circ", None, None),
        P("ax", "circ", None, None),
        P("ax", "circ", None, None),
    )
    return jax.shard_map(
        per_device,
        mesh=mesh,
        in_specs=placed,
        out_specs=P(None, "circ", "ax", None),
        check_vma=False,
    )
```

```python
import functools

import jax
import jax.numpy as jnp
from jax import lax
from jax.experimental import pallas as pl
from jax.experimental.pallas import tpu as pltpu
from jax.sharding import PartitionSpec as P


def extended(block, sides, width, periodic):
    for axis, dim in sides:
        count = lax.axis_size(axis)
        forward = [(i, i + 1) for i in range(count - 1)]
        if periodic:
            forward.append((count - 1, 0))
        backward = [(target, source) for source, target in forward]
        low = lax.ppermute(
            lax.slice_in_dim(block, block.shape[dim] - width, None, axis=dim), axis, forward
        )
        high = lax.ppermute(lax.slice_in_dim(block, 0, width, axis=dim), axis, backward)
        block = jnp.concatenate([low, block, high], axis=dim)
    return block


def scan_forward(coef, value, pos):
    points = value.shape[-1]
    shift = 1
    while shift < points:
        keep = pos >= shift
        value = value + coef * jnp.where(keep, pltpu.roll(value, shift, 2), 0.0)
        coef = coef * pltpu.roll(coef, shift, 2)
        shift *= 2
    return value


def scan_backward(coef, value, pos):
    points = value.shape[-1]
    shift = 1
    while shift < points:
        keep = pos < points - shift
        value = value + coef * jnp.where(keep, pltpu.roll(value, points - shift, 2), 0.0)
        coef = coef * pltpu.roll(coef, points - shift, 2)
        shift *= 2
    return value


MESH = pl.DeviceIdType.MESH


def solve_rows(rhs, lower, upper, pivot):
    fields, rows, points = rhs.shape
    pos = lax.broadcasted_iota(jnp.int32, (fields, rows, points), 2)
    active = rhs == rhs
    forward_coef = jnp.where(active, -lower.astype(jnp.float32), 0.0)
    interim = scan_forward(forward_coef, jnp.where(active, rhs, 0.0), pos)
    applied = []
    for f in range(fields):
        total = pivot[f * fields].astype(jnp.float32) * interim[0]
        for g in range(1, fields):
            total = total + pivot[f * fields + g].astype(jnp.float32) * interim[g]
        applied.append(total)
    applied = jnp.stack(applied, axis=0)
    backward_coef = jnp.where(active, -upper.astype(jnp.float32), 0.0)
    return scan_backward(backward_coef, jnp.where(active, applied, 0.0), pos)


def owner_kernel(
    peers, group, rhs_ref, lower_ref, upper_ref, pivot_ref, out_ref,
    rhs_in, solved, lower_v, upper_v, pivot_v,
    send_rhs, recv_rhs, send_sol, recv_sol, local_sems,
):
    width = rhs_ref.shape[0] // peers
    fields, _, points = lower_ref.shape
    groups = peers // group
    rows = group * width
    me = lax.axis_index("circ")
    plane = lax.axis_index("ax")
    mine = me // group
    factor_copies = [
        pltpu.make_async_copy(lower_ref, lower_v, local_sems.at[0]),
        pltpu.make_async_copy(upper_ref, upper_v, local_sems.at[1]),
        pltpu.make_async_copy(pivot_ref, pivot_v, local_sems.at[2]),
    ]
    for copy in factor_copies:
        copy.start()
    barrier = pltpu.get_barrier_semaphore()

    def greet(i, carry):
        peer = lax.rem(me + i, peers)
        pl.semaphore_signal(barrier, inc=1, device_id=(peer, plane), device_id_type=MESH)
        return carry

    lax.fori_loop(1, peers, greet, 0)
    pl.semaphore_wait(barrier, peers - 1)

    def window(index):
        return pl.ds(index * width, width)

    def rhs_copy(source, target):
        return pltpu.make_async_remote_copy(
            src_ref=rhs_ref.at[window(target)],
            dst_ref=rhs_in.at[window(source)],
            send_sem=send_rhs.at[target],
            recv_sem=recv_rhs.at[source],
            device_id=(lax.select(source == me, target, source), plane),
            device_id_type=MESH,
        )

    def sol_copy(source, target):
        return pltpu.make_async_remote_copy(
            src_ref=solved.at[window(target)],
            dst_ref=out_ref.at[window(source)],
            send_sem=send_sol.at[target],
            recv_sem=recv_sol.at[source],
            device_id=(lax.select(source == me, target, source), plane),
            device_id_type=MESH,
        )

    own_rhs = pltpu.make_async_copy(rhs_ref.at[window(me)], rhs_in.at[window(me)], local_sems.at[3])
    own_sol = pltpu.make_async_copy(solved.at[window(me)], out_ref.at[window(me)], local_sems.at[4])

    def order(step):
        quarter, kind = step // 4, step % 4
        near = lax.select(kind == 0, quarter, groups - 1 - quarter)
        far = lax.select(kind == 2, groups // 4 + quarter, 3 * groups // 4 - 1 - quarter)
        return lax.select(kind < 2, near, far)

    def send(i, carry):
        target = group * lax.rem(mine - order(i // group) + groups, groups) + i % group

        @pl.when(target == me)
        def _():
            own_rhs.start()

        @pl.when(target != me)
        def _():
            rhs_copy(me, target).start()

        return carry

    lax.fori_loop(0, peers, send, 0)
    for copy in factor_copies:
        copy.wait()

    def solve(j, carry):
        g = lax.rem(mine + order(j), groups)
        for r in range(group):
            source = g * group + r

            @pl.when(source == me)
            def _():
                own_rhs.wait()

            @pl.when(source != me)
            def _():
                rhs_copy(source, me).wait_recv()

        block = pl.ds(pl.multiple_of(g * rows, rows), rows)
        by_field = [pl.ds(f * points, points) for f in range(fields)]
        rhs = jnp.stack([rhs_in[block, lanes] for lanes in by_field], axis=0)
        result = solve_rows(rhs, lower_v[:, block, :], upper_v[:, block, :], pivot_v[:, block, :])
        for f, lanes in enumerate(by_field):
            solved[block, lanes] = result[f]
        for r in range(group):
            target = g * group + r

            @pl.when(target == me)
            def _():
                own_sol.start()

            @pl.when(target != me)
            def _():
                sol_copy(me, target).start()

        return carry

    lax.fori_loop(0, groups, solve, 0)

    def finish(i, carry):
        peer = lax.rem(me + i, peers)
        rhs_copy(me, peer).wait_send()
        sol_copy(me, peer).wait_send()
        sol_copy(peer, me).wait_recv()
        return carry

    lax.fori_loop(1, peers, finish, 0)
    own_sol.wait()


def owner_solve(rhs, lower, upper, pivot, peers, group=4):
    return pl.pallas_call(
        functools.partial(owner_kernel, peers, group),
        out_shape=jax.ShapeDtypeStruct(rhs.shape, rhs.dtype),
        in_specs=[pl.BlockSpec(memory_space=pl.ANY)] * 4,
        out_specs=pl.BlockSpec(memory_space=pl.ANY),
        scratch_shapes=[
            pltpu.VMEM(rhs.shape, jnp.float32),
            pltpu.VMEM(rhs.shape, jnp.float32),
            pltpu.VMEM(lower.shape, lower.dtype),
            pltpu.VMEM(upper.shape, upper.dtype),
            pltpu.VMEM(pivot.shape, pivot.dtype),
            pltpu.SemaphoreType.DMA((peers,)),
            pltpu.SemaphoreType.DMA((peers,)),
            pltpu.SemaphoreType.DMA((peers,)),
            pltpu.SemaphoreType.DMA((peers,)),
            pltpu.SemaphoreType.DMA((5,)),
        ],
        compiler_params=pltpu.CompilerParams(
            collective_id=0, has_side_effects=True, vmem_limit_bytes=48 * 1024 * 1024
        ),
    )(rhs, lower, upper, pivot)


def per_device(
    adjoint, source, step_size, lengths, line_owner, coupling, lower_coef, upper_coef, pivot_inverse
):
    fields, circ_cells, axial_cells, points = adjoint.shape
    line_count = circ_cells * axial_cells
    circ_devices = lax.axis_size("circ")
    capacity = 2 * line_count // circ_devices
    slot_count = lower_coef.shape[1]
    circ_padded = extended(adjoint, (("circ", 1),), 1, True)
    axial_padded = extended(adjoint, (("ax", 2),), 1, False)
    neighbours = (
        circ_padded[:, 2:],
        circ_padded[:, :-2],
        axial_padded[:, :, 2:],
        axial_padded[:, :, :-2],
    )
    coupled = None
    for k, near in enumerate(neighbours):
        for g in range(fields):
            term = coupling[k, :, g][:, None, None, None] * near[g][None]
            coupled = term if coupled is None else coupled + term
    residual = source - adjoint + step_size[None] * coupled
    active = jnp.arange(points)[None, None, None, :] < lengths[None, :, :, None]
    residual = jnp.where(active, residual, jnp.nan)
    line_rhs = residual.transpose(1, 2, 0, 3).reshape(line_count, fields * points)
    targets = line_owner.reshape(line_count)
    ordinal = jnp.arange(line_count)
    earlier_same = (targets[:, None] == targets[None, :]) & (ordinal[None, :] < ordinal[:, None])
    slot_ids = targets * capacity + jnp.sum(earlier_same, axis=1)
    line_of_slot = jnp.full((slot_count,), line_count, jnp.int32).at[slot_ids].set(
        ordinal.astype(jnp.int32)
    )
    padded_rhs = jnp.concatenate(
        [line_rhs, jnp.full((1, fields * points), jnp.nan, jnp.float32)], axis=0
    )
    outgoing = jnp.take(padded_rhs, line_of_slot, axis=0, mode="clip")
    returned = owner_solve(
        outgoing,
        lower_coef[0].transpose(1, 0, 2),
        upper_coef[0].transpose(1, 0, 2),
        pivot_inverse[0].transpose(1, 0, 2),
        circ_devices,
    )
    correction = jnp.take(returned, slot_ids, axis=0, mode="clip")
    correction = correction.reshape(circ_cells, axial_cells, fields, points).transpose(2, 0, 1, 3)
    return adjoint + correction


def solution(mesh):
    placed = (
        P(None, "circ", "ax", None),
        P(None, "circ", "ax", None),
        P("circ", "ax", None),
        P("circ", "ax"),
        P("ax", "circ", None, None),
        P(),
        P("ax", "circ", None, None),
        P("ax", "circ", None, None),
        P("ax", "circ", None, None),
    )
    return jax.shard_map(
        per_device,
        mesh=mesh,
        in_specs=placed,
        out_specs=P(None, "circ", "ax", None),
        check_vma=False,
    )
```
